256 devices in a mesh: gz: 64 (over x, z, y_hi), gx: 4 (over y_lo, core).
Axes of the slice: x: 4, y: 4 (y_hi: 2, y_lo: 2; y = y_hi * 2 + y_lo), z: 8, core: 2. Of those that a mesh axis runs over, the one named last changes fastest.
Arguments:
- velocity: float32 [3, 1024, 64, 128], P(None, 'gz', 'gx'), may hold values from -6 to 6
- pressure: float32 [1024, 64, 128], P('gz', 'gx'), may hold values from -6 to 6
- void_fraction: float32 [1024, 64, 128], P('gz', 'gx'), may hold values from 0.4 to 0.95
- history: float32 [2, 3, 1024, 64, 128], P(None, None, 'gz', 'gx'), may hold values from -6 to 6
- remap_list: int32 [64, 4, 8], replicated, may hold values from 0 to 23, as said below
- parcel_records: float32 [16, 1048576], P(None, ('gz', 'gx')), may hold values from -1 to 1
- parcel_owner: int32 [1048576, 1], P(('gz', 'gx')), may hold values from 0 to 63; in each aligned block of 4096 rows (0 to 4095, 4096 to 8191, ...) at most 128 rows name the same one
- parcel_cells: int32 [1048576], P(('gz', 'gx')), may hold values from 0 to 32767
Outputs:
- new_velocity: float32 [3, 1024, 64, 128], P(None, 'gz', 'gx')
- new_pressure: float32 [1024, 64, 128], P('gz', 'gx')
- new_history: float32 [2, 3, 1024, 64, 128], P(None, None, 'gz', 'gx')
The draws below stay inside these ranges and needn't reach their ends.
Inputs may be any that keep to these rules, and one draw needn't show every extreme that they name: `remap_list`: entries are (o + 1) * 8 + s with o in -1, 0, 1; the new bricks are a permutation of the old ones, and in every draw exactly 1 new bricks of each device come from each of its two neighbours along gz (o = -1 and o = +1). `parcel_owner`: of the 4096 parcels of one device, at most 128 have the same owner.
All inputs are finite; a program needn't handle non-finite values.
Results may differ from the reference program's by a relative error of at most 0.00012.
Values sent between devices are 32-bit elements; how exact they have to be, the bound alone decides.
No kernel may reach another device: no remote copies, remote signals or barrier semaphores. Data moves between devices by JAX's collectives and lax.ppermute only.
A program may use at most 128 MiB of HBM per device.

```python
import math
import jax
import jax.numpy as jnp
import numpy as np

BRICK = 16
BRICKS_DEV = 8
MOVE = 1
SWEEPS = 6
REC = 16
PDEV = 4096
NZ = 1024
NX = 64
NY = 128
CELLS_DEV = 32768
PARCELS = 1048576
CAP = 128
N_GZ = 64
N_GX = 4


def draw_remap_list(key, part):
    first_key, second_key = jax.random.split(key)
    devices = N_GZ * N_GX
    orders = jax.vmap(lambda subkey: jax.random.permutation(subkey, BRICKS_DEV))(jax.random.split(first_key, devices))
    orders = orders.reshape(N_GZ, N_GX, BRICKS_DEV).astype(jnp.int32)
    from_below = jnp.roll(orders, 1, axis=0)[:, :, :MOVE]
    from_above = jnp.roll(orders, -1, axis=0)[:, :, MOVE:2 * MOVE]
    staying = orders[:, :, 2 * MOVE:]
    codes = jnp.concatenate([from_below, BRICKS_DEV + staying, 2 * BRICKS_DEV + from_above], axis=2)
    shuffle = jax.vmap(lambda subkey: jax.random.permutation(subkey, BRICKS_DEV))(jax.random.split(second_key, devices))
    shuffle = shuffle.reshape(N_GZ, N_GX, BRICKS_DEV).astype(jnp.int32)
    return jnp.take_along_axis(codes, shuffle, axis=2).astype(jnp.int32)


def touch_ends(drawn, stream_key, smallest, high):
    extent = drawn.shape
    index_at = [jax.random.randint(jax.random.fold_in(stream_key, axis), (), 0, extent[axis]) for axis in range(len(extent))]
    drawn = drawn.at[tuple(index_at)].set(smallest)
    longest = extent.index(max(extent))
    index_at[longest] = (index_at[longest] + 1) % extent[longest]
    return drawn.at[tuple(index_at)].set(high)


def block_scale(stream_key, dims, shards, low, high):
    level, own = 1.0, jax.random.fold_in(stream_key, 6)
    for axis_at, parts in shards:
        draws = jnp.exp(jax.random.uniform(jax.random.fold_in(own, axis_at), (parts,), jnp.float32, low / len(shards), high / len(shards)))
        level = level * jnp.repeat(draws, dims[axis_at] // parts).reshape([-1 if axis == axis_at else 1 for axis in range(len(dims))])
    return level


def assign_block(stream_key, own, number, rows, count, top, reach, skew):
    ranking = jax.random.permutation(stream_key, count)
    heavy_load, ordinary = shares(count, rows * top, reach, skew, True), shares(count, rows * top, reach, skew, False)
    places = jnp.arange(count)

    def named(tallies, rotation):
        used = int((tallies > 0).sum())
        fixed = max(1, used // 4)
        passed = fixed + (places - fixed + rotation * (used - fixed)) % max(1, count - fixed)
        return jnp.zeros((count,), jnp.int32).at[ranking[jnp.where(places < fixed, places, passed)]].set(jnp.asarray(tallies, jnp.int32))

    tallies = jnp.where(number % 4 == 0, named(heavy_load, number // 4), named(ordinary, number - number // 4 - 1))
    mixed = jax.random.permutation(jax.random.fold_in(own, 3), count)
    donor, taker = mixed[0:count // 2 * 2:2], mixed[1:count // 2 * 2:2]
    room = jnp.minimum(tallies[donor] - 1, reach - tallies[taker]) // 2
    room = jnp.where((donor == ranking[0]) | (taker == ranking[0]) | (tallies[taker] == 0), 0, jnp.maximum(room, 0))
    passed = jax.random.randint(jax.random.fold_in(own, 4), (count // 2,), 0, 1 << 20) % (room + 1)
    tallies = tallies.at[donor].add(-passed).at[taker].add(passed)
    members = jnp.searchsorted(jnp.cumsum(tallies), jnp.arange(rows * top), side="right").astype(jnp.int32)
    grid = members.reshape(top, rows).T
    grid = grid[jax.random.permutation(jax.random.fold_in(own, 1), rows)]
    rotation = jax.random.randint(jax.random.fold_in(own, 2), (rows, 1), 0, top)
    return jnp.take_along_axis(grid, (jnp.arange(top)[None, :] + rotation) % top, axis=1)


def shares(number_of, total, bound, lean, full):
    portions = [(1 << 20) // math.isqrt(standing ** lean) + 1 for standing in range(1, number_of + 1)]
    largest = bound if full else min(bound, max(-(-total // number_of), total * portions[0] // sum(portions)))
    least = 1 if total - largest >= number_of - 1 else 0
    holding, spare = [largest] + [least] * (number_of - 1), total - largest - least * (number_of - 1)
    while spare > 0:
        free = [i for i in range(1, number_of) if holding[i] < largest] or [i for i in range(1, number_of) if holding[i] < bound]
        mass, budget = sum([portions[i] for i in free]), spare
        for i in free:
            more = min(bound - holding[i], max(1, budget * portions[i] // mass), spare)
            holding[i] = holding[i] + more
            spare = spare - more
    return np.array(holding)


def gaussian(key, extent, deviation, limit, cuts=(), kind=jnp.bfloat16):
    values = jax.random.normal(key, extent, jnp.float32) * deviation
    if len(cuts) > 0:
        values = block_scale(key, extent, cuts, -0.22, 0.18) * values
    return jnp.clip(values, min=-limit, max=limit).astype(kind)


def setup_inputs(seed: int = 0) -> dict:
    seeds = jax.random.split(jax.random.key(seed), 9)
    velocity = gaussian(seeds[0], (3, NZ, NX, NY), 1.0, 6.0, ((1, 64), (2, 4)), jnp.float32)
    pressure = gaussian(seeds[1], (NZ, NX, NY), 1.0, 6.0, ((0, 64), (1, 4)), jnp.float32)
    void_fraction = jnp.clip(0.4 + 0.54999998 * jax.random.uniform(seeds[2], (NZ, NX, NY), jnp.float32) ** block_scale(seeds[2], (NZ, NX, NY), ((0, 64), (1, 4)), -0.2, 0.2), 0.4, 0.95)
    history = gaussian(seeds[3], (2, 3, NZ, NX, NY), 1.0, 6.0, ((2, 64), (3, 4)), jnp.float32)
    remap_list = draw_remap_list(jax.random.fold_in(seeds[8], 71), 0)
    parcel_records = jnp.clip(jax.random.uniform(seeds[5], (REC, PARCELS), jnp.float32, -1.0, 1.0) * block_scale(seeds[5], (REC, PARCELS), ((1, 256),), -0.4, 0.0), -1.0, 1.0)
    parcel_owner_keys = jax.random.split(jax.random.fold_in(seeds[6], 1), PARCELS // PDEV)
    parcel_owner_turns = jax.random.permutation(jax.random.fold_in(seeds[6], 3), PARCELS // PDEV)
    parcel_owner = jax.vmap(lambda own, number: assign_block(jax.random.fold_in(seeds[6], 2), own, number, PDEV, N_GZ, 1, CAP, 2))(parcel_owner_keys, parcel_owner_turns).reshape((PARCELS, 1))
    parcel_cells = touch_ends(jax.random.randint(seeds[7], (PARCELS,), 0, CELLS_DEV), jax.random.fold_in(seeds[7], 1), 0, CELLS_DEV - 1).astype(jnp.int32)
    return {"velocity": velocity, "pressure": pressure, "void_fraction": void_fraction, "history": history, "remap_list": remap_list, "parcel_records": parcel_records, "parcel_owner": parcel_owner, "parcel_cells": parcel_cells}


TIME_STEP = 0.25
VISCOSITY = 0.5
DRAG_SCALE = 0.5
RELAXATION = 0.8
WEIGHT_NEW = 23.0 / 12.0
WEIGHT_LAST = 16.0 / 12.0
WEIGHT_OLDER = 5.0 / 12.0


def remap_field(field, remap_list):
    components = field.shape[0]
    blocks = field.reshape(components, N_GZ, BRICK, N_GX, BRICK, BRICKS_DEV, BRICK).transpose(1, 3, 5, 0, 2, 4, 6)
    offset = remap_list // BRICKS_DEV - 1
    source_slot = remap_list % BRICKS_DEV
    cycle_source = (jnp.arange(N_GZ, dtype=jnp.int32)[:, None, None] + offset + N_GZ) % N_GZ
    line_source = jnp.broadcast_to(jnp.arange(N_GX, dtype=jnp.int32)[None, :, None], remap_list.shape)
    moved = blocks[cycle_source, line_source, source_slot]
    return moved.transpose(3, 0, 4, 1, 5, 2, 6).reshape(field.shape)


def neighbour_of(field):
    def neighbour(number):
        if number == 0:
            return jnp.roll(field, -1, axis=1)
        if number == 1:
            return jnp.roll(field, 1, axis=1)
        if number == 2:
            return jnp.concatenate([field[:, :, 1:], jnp.zeros_like(field[:, :, :1])], axis=2)
        if number == 3:
            return jnp.concatenate([jnp.zeros_like(field[:, :, :1]), field[:, :, :-1]], axis=2)
        if number == 4:
            return jnp.concatenate([field[..., 1:], jnp.zeros_like(field[..., :1])], axis=3)
        return jnp.concatenate([jnp.zeros_like(field[..., :1]), field[..., :-1]], axis=3)
    return neighbour


def parcel_terms(records):
    classes = records.reshape(records.shape[0] // 4, 4, records.shape[-1])
    coefficient = DRAG_SCALE * jnp.exp(classes[:, 3])
    momentum = jnp.sum(coefficient[:, None] * classes[:, :3], axis=0)
    total = jnp.sum(coefficient, axis=0)
    return jnp.concatenate([momentum, total[None]], axis=0)


def momentum_rate(flow, flow_near, void, conduct, deposit):
    laplace = conduct[0] * (flow_near(0) - flow)
    for number in range(1, 6):
        laplace = laplace + conduct[number] * (flow_near(number) - flow)
    return (VISCOSITY * laplace + deposit[0:3] - deposit[3:4] * flow) / void


def divergence(trial, trial_near, conduct):
    total = None
    for axis_no in range(3):
        part = trial[axis_no:axis_no + 1]
        term = 0.5 * (conduct[2 * axis_no] * (part + trial_near(2 * axis_no)[axis_no:axis_no + 1])
                      - conduct[2 * axis_no + 1] * (part + trial_near(2 * axis_no + 1)[axis_no:axis_no + 1]))
        total = term if axis_no == 0 else total + term
    return total


def relax(press, press_near, conduct, weight, source):
    applied = weight * press
    for number in range(6):
        applied = applied - conduct[number] * press_near(number)
    return press + RELAXATION * (source - applied) / weight


def correct(trial, press, press_near, conduct, void):
    pieces = []
    for axis_no in range(3):
        slope = 0.5 * (conduct[2 * axis_no] * (press_near(2 * axis_no) - press)
                       + conduct[2 * axis_no + 1] * (press - press_near(2 * axis_no + 1)))
        pieces.append(trial[axis_no:axis_no + 1] - TIME_STEP * slope / void)
    return jnp.concatenate(pieces, axis=0)


def reference(velocity, pressure, void_fraction, history, remap_list, parcel_records, parcel_owner, parcel_cells):
    flow = remap_field(velocity, remap_list)
    latest = remap_field(history[0], remap_list)
    older = remap_field(history[1], remap_list)
    press = remap_field(pressure[None], remap_list)
    void = remap_field(void_fraction[None], remap_list)
    owners = parcel_owner[:, 0]
    parcel_rows = jnp.arange(PARCELS, dtype=jnp.int32)
    column_dev = (parcel_rows // PDEV) % N_GX
    depth_pos = parcel_cells // (BRICK * NY)
    across_pos = (parcel_cells // NY) % BRICK
    length_pos = parcel_cells % NY
    deposit = jnp.zeros((4, NZ, NX, NY), jnp.float32).at[
        :, owners * BRICK + depth_pos, column_dev * BRICK + across_pos, length_pos].add(parcel_terms(parcel_records))
    void_near = neighbour_of(void)
    conduct = [void * void_near(number) for number in range(6)]
    weight = conduct[0]
    for number in range(1, 6):
        weight = weight + conduct[number]
    rate = momentum_rate(flow, neighbour_of(flow), void, conduct, deposit)
    trial = flow + TIME_STEP * (WEIGHT_NEW * rate - WEIGHT_LAST * latest + WEIGHT_OLDER * older)
    source = -divergence(trial, neighbour_of(trial), conduct) / TIME_STEP
    for repeat in range(SWEEPS):
        press = relax(press, neighbour_of(press), conduct, weight, source)
    final = correct(trial, press, neighbour_of(press), conduct, void)
    return final, press[0], jnp.stack([rate, latest], axis=0)
```

```python
import jax
import jax.numpy as jnp
from jax import lax
from jax.experimental import pallas as pl
from jax.experimental.pallas import tpu as pltpu
from jax.sharding import PartitionSpec as P

SWEEPS = 6
TIME_STEP = 0.25
VISCOSITY = 0.5
DRAG_SCALE = 0.5
RELAXATION = 0.8
WEIGHT_NEW = 23.0 / 12.0
WEIGHT_LAST = 16.0 / 12.0
WEIGHT_OLDER = 5.0 / 12.0

BRICK = 16
BRICKS = 8
EDGE = 16
LANES = 128
ROWS = 8
HALO = SWEEPS + 1
WIDE = HALO + EDGE + HALO
REACH = SWEEPS
SPAN = REACH + EDGE + REACH
FIELDS = 11
OWNERS = 64
CAP = 128
PARCELS = 4096
BLOCK = 256
VMEM_LIMIT = 48 * 1024 * 1024

F32 = jnp.float32
BF16 = jnp.bfloat16


def call(kernel, outs, args, smem=(), scratch=()):
    specs = [
        pl.BlockSpec(memory_space=pltpu.SMEM if number in smem else pltpu.VMEM)
        for number in range(len(args))
    ]
    return pl.pallas_call(
        kernel,
        out_shape=[jax.ShapeDtypeStruct(shape, F32) for shape in outs],
        in_specs=specs,
        out_specs=[pl.BlockSpec(memory_space=pltpu.VMEM) for _ in outs],
        scratch_shapes=list(scratch),
        compiler_params=pltpu.CompilerParams(vmem_limit_bytes=VMEM_LIMIT),
    )(*args)


def lane_of():
    return lax.broadcasted_iota(jnp.int32, (ROWS, LANES), 1)


def take(block, index):
    return jnp.take_along_axis(block, index, axis=1, mode="promise_in_bounds")


def field_block(refs, field, tile):
    velocity, history, pressure, void = refs
    layer, half = tile // 2, tile % 2
    rows = slice(half * ROWS, (half + 1) * ROWS)
    if field < 3:
        return velocity[field, layer, rows, :]
    if field < 9:
        return history[(field - 3) // 3, field % 3, layer, rows, :]
    return (pressure if field == 9 else void)[layer, rows, :]


def pack_kernel(codes, velocity, history, pressure, void, to_upper, to_lower):
    cycle = lax.axis_index("gz")
    line = lax.axis_index("gx")
    size = lax.axis_size("gz")
    upper = lax.rem(cycle + 1, size)
    lower = lax.rem(cycle + size - 1, size)
    slot_up = jnp.int32(0)
    slot_down = jnp.int32(0)
    for brick in range(BRICKS):
        code = codes[line * BRICKS + brick, upper]
        slot_up = slot_up + jnp.where(code < BRICKS, code, 0)
        code = codes[line * BRICKS + brick, lower]
        slot_down = slot_down + jnp.where(code >= 2 * BRICKS, code - 2 * BRICKS, 0)
    lane = lane_of()
    group = lane // BRICK
    index_up = slot_up * BRICK + lane % BRICK
    index_down = slot_down * BRICK + lane % BRICK
    refs = (velocity, history, pressure, void)
    for field in range(FIELDS):
        for part in range(4):
            up = jnp.zeros((ROWS, LANES), F32)
            down = jnp.zeros((ROWS, LANES), F32)
            for place in range(8):
                block = field_block(refs, field, part * 8 + place)
                up = jnp.where(group == place, take(block, index_up), up)
                down = jnp.where(group == place, take(block, index_down), down)
            row = (field * 4 + part) * ROWS
            to_upper[row : row + ROWS, :] = up
            to_lower[row : row + ROWS, :] = down


def remap_kernel(
    codes, velocity, history, pressure, void, lower, upper,
    flow_out, latest_out, base_out, press_out, void_out, to_upper, to_lower,
):
    cycle = lax.axis_index("gz")
    line = lax.axis_index("gx")
    lane = lane_of()
    group = lane // BRICK
    code_of = jnp.zeros((ROWS, LANES), jnp.int32)
    for brick in range(BRICKS):
        code_of = jnp.where(group == brick, codes[line * BRICKS + brick, cycle], code_of)
    from_lower = code_of < BRICKS
    from_upper = code_of >= 2 * BRICKS
    index_own = (code_of % BRICKS) * BRICK + lane % BRICK
    refs = (velocity, history, pressure, void)
    for tile in range(32):
        part, place = tile // 8, tile % 8
        index_in = place * BRICK + lane % BRICK
        layer, half = tile // 2, tile % 2
        rows = slice(half * ROWS, (half + 1) * ROWS)
        moved = []
        for field in range(FIELDS):
            row = (field * 4 + part) * ROWS
            own = take(field_block(refs, field, tile), index_own)
            low = take(lower[row : row + ROWS, :], index_in)
            high = take(upper[row : row + ROWS, :], index_in)
            moved.append(jnp.where(from_lower, low, jnp.where(from_upper, high, own)))
        press, void_new = moved[9], moved[10]
        press_out[layer, rows, :] = press
        void_out[layer, rows, :] = void_new
        for axis_no in range(3):
            flow, latest, older = moved[axis_no], moved[3 + axis_no], moved[6 + axis_no]
            flow_out[axis_no, layer, rows, :] = flow
            latest_out[axis_no, layer, rows, :] = latest
            base_out[axis_no, layer, rows, :] = flow + TIME_STEP * (
                WEIGHT_OLDER * older - WEIGHT_LAST * latest
            )
            if layer == 0:
                to_lower[2 * HALO + axis_no, rows, :] = void_new * flow
            if layer == EDGE - 1:
                to_upper[2 * HALO + axis_no, rows, :] = void_new * flow
        if layer < HALO:
            to_lower[layer, rows, :] = void_new
            to_lower[HALO + layer, rows, :] = press
        if layer >= EDGE - HALO:
            to_upper[layer - EDGE + HALO, rows, :] = void_new
            to_upper[2 * HALO + layer - EDGE, rows, :] = press


def pack_rows_kernel(flow, press, void, lower, upper, to_right, to_left):
    for send, rows, edge in ((to_right, slice(8, 16), EDGE - 1), (to_left, slice(0, 8), 0)):
        for number, own in ((0, void), (1, press)):
            start = number * WIDE * ROWS
            for layer in range(HALO):
                row = start + layer * ROWS
                send[row : row + ROWS, :] = lower[number * HALO + layer, rows, :]
                row = start + (HALO + EDGE + layer) * ROWS
                send[row : row + ROWS, :] = upper[number * HALO + layer, rows, :]
            for layer in range(EDGE):
                row = start + (HALO + layer) * ROWS
                send[row : row + ROWS, :] = own[layer, rows, :]
        for axis_no in range(3):
            row = 2 * WIDE * ROWS + axis_no * EDGE
            send[row : row + EDGE, :] = void[:, edge, :] * flow[axis_no, :, edge, :]


def split_two(value):
    high = value.astype(BF16)
    return high, (value - high.astype(F32)).astype(BF16)


NT = (((1,), (1,)), ((), ()))


def dispatch_kernel(records, owners, cells, out, shown, total):
    blocks = PARCELS // BLOCK
    owner_iota = lax.broadcasted_iota(jnp.int32, (OWNERS, BLOCK), 0)
    before = (
        lax.broadcasted_iota(jnp.int32, (BLOCK, BLOCK), 0)
        < lax.broadcasted_iota(jnp.int32, (BLOCK, BLOCK), 1)
    ).astype(F32).astype(BF16)

    def row_of(ref, block):
        return jnp.concatenate([ref[2 * block : 2 * block + 1, :], ref[2 * block + 1 : 2 * block + 2, :]], axis=1)

    for block in range(blocks):
        hit = (row_of(owners, block) == owner_iota).astype(F32)
        shown[block * OWNERS : (block + 1) * OWNERS, :] = hit.astype(BF16)
    earlier = lax.dot_general(
        shown[...], before, (((1,), (0,)), ((), ())), preferred_element_type=F32
    )
    base = jnp.zeros((OWNERS, 1), F32)
    row_iota = lax.broadcasted_iota(jnp.int32, (4, BLOCK), 0)
    key_iota = lax.broadcasted_iota(jnp.int32, (2 * CAP, BLOCK), 0)
    total[...] = jnp.zeros_like(total)
    for block in range(blocks):
        rows = slice(block * OWNERS, (block + 1) * OWNERS)
        hit = shown[rows, :].astype(F32)
        seen = earlier[block * OWNERS : (block + 1) * OWNERS, :]
        rank = jnp.sum(hit * (seen + base), axis=0, keepdims=True).astype(jnp.int32)
        base = base + seen[:, BLOCK - 1 : BLOCK] + hit[:, BLOCK - 1 : BLOCK]
        owner = row_of(owners, block)
        cell = row_of(cells, block)
        key = (owner // 32) * CAP + rank
        placed = (key == key_iota).astype(F32).astype(BF16)
        lanes = slice(block * BLOCK, (block + 1) * BLOCK)
        terms = jnp.zeros((4, BLOCK), F32)
        for size_class in range(4):
            state = records[4 * size_class : 4 * size_class + 4, lanes]
            coefficient = DRAG_SCALE * jnp.exp(state[3:4, :])
            terms = terms + coefficient * jnp.where(row_iota == 3, 1.0, state)
        depth, across, along = cell // 2048, (cell // LANES) % EDGE, cell % LANES
        major = (depth * 8 + across % 8).astype(F32)
        minor = ((across // 8) * LANES + along).astype(F32)
        blank2 = jnp.zeros((2, BLOCK), F32)
        blank4 = jnp.zeros((4, BLOCK), F32)
        coarse = terms.astype(BF16).astype(F32)
        values = jnp.concatenate(
            [coarse, major, minor, blank2, terms - coarse, blank4], axis=0
        ).astype(BF16)
        group = jnp.broadcast_to(owner % 32, (16, BLOCK)).astype(F32).astype(BF16)
        spread = jnp.concatenate(
            [jnp.where(group == jnp.asarray(number, BF16), values, jnp.zeros_like(values)) for number in range(32)],
            axis=0,
        )
        total[...] += lax.dot_general(spread, placed, NT, preferred_element_type=F32)
    for owner in range(OWNERS):
        row = (owner % 32) * 16
        lanes = slice((owner // 32) * CAP, (owner // 32 + 1) * CAP)
        out[owner, :, :] = total[row : row + 8, lanes] + total[row + 8 : row + 16, lanes]


def deposit_kernel(arrived, out, total):
    step = 4
    width = step * CAP
    iota_major = lax.broadcasted_iota(jnp.int32, (128, width), 0).astype(F32).astype(BF16)
    iota_minor = lax.broadcasted_iota(jnp.int32, (256, width), 0).astype(F32).astype(BF16)
    total[...] = jnp.zeros_like(total)
    zero = jnp.zeros((128, width), BF16)

    def body(number, carry):
        def row_of(channel):
            return jnp.concatenate(
                [arrived[number * step + source, channel : channel + 1, :] for source in range(step)], axis=1
            )

        major = jnp.broadcast_to(row_of(4), (128, width)).astype(BF16)
        minor = jnp.broadcast_to(row_of(5), (256, width)).astype(BF16)
        placed = jnp.where(minor == iota_minor, jnp.ones((256, width), BF16), jnp.zeros((256, width), BF16))
        here = major == iota_major
        for channel in range(4):
            value = row_of(channel)
            coarse = value.astype(BF16).astype(F32)
            for part, piece in ((0, coarse), (1, value - coarse)):
                spread = jnp.where(here, jnp.broadcast_to(piece, (128, width)).astype(BF16), zero)
                row = (channel * 2 + part) * 128
                total[row : row + 128, :] += lax.dot_general(spread, placed, NT, preferred_element_type=F32)
        return carry

    lax.fori_loop(0, OWNERS // step, body, 0)
    for channel in range(4):
        row = channel * 256
        for half in range(2):
            lanes = slice(half * LANES, (half + 1) * LANES)
            summed = total[row : row + 128, lanes] + total[row + 128 : row + 256, lanes]
            out[channel, :, half * ROWS : (half + 1) * ROWS, :] = summed.reshape(EDGE, ROWS, LANES)


def lane_up(value):
    lane = lax.broadcasted_iota(jnp.int32, value.shape, 1)
    return jnp.where(lane == LANES - 1, 0.0, pltpu.roll(value, LANES - 1, 1))


def lane_down(value):
    lane = lax.broadcasted_iota(jnp.int32, value.shape, 1)
    return jnp.where(lane == 0, 0.0, pltpu.roll(value, 1, 1))


def row_up(value, after):
    count = value.shape[0]
    row = lax.broadcasted_iota(jnp.int32, value.shape, 0)
    return jnp.where(row == count - 1, after, pltpu.roll(value, count - 1, 0))


def row_down(value, before):
    row = lax.broadcasted_iota(jnp.int32, value.shape, 0)
    return jnp.where(row == 0, before, pltpu.roll(value, 1, 0))


M_LOW = 2 * HALO
M_ROWS = 2 * WIDE * ROWS


def rate_kernel(
    flow, latest, base, void, lower, upper, left, right, deposit,
    history_out, trial_out, div_out, to_upper, to_lower, edge_out, scaled,
):
    def void_layer(layer):
        if layer < 0:
            return lower[HALO + layer, :, :]
        if layer >= EDGE:
            return upper[layer - EDGE, :, :]
        return void[layer, :, :]

    def moment_layer(axis_no, layer):
        if layer < 0:
            return lower[M_LOW + axis_no, :, :]
        if layer >= EDGE:
            return upper[M_LOW + axis_no, :, :]
        return void[layer, :, :] * flow[axis_no, layer, :, :]

    for layer in range(EDGE):
        own = void[layer, :, :]
        row = (HALO + layer) * ROWS
        void_left = left[row + ROWS - 1 : row + ROWS, :]
        void_right = right[row : row + 1, :]
        near = (
            void_layer(layer + 1), void_layer(layer - 1),
            row_up(own, void_right), row_down(own, void_left),
            lane_up(own), lane_down(own),
        )
        around = near[0] + near[1] + near[2] + near[3] + near[4] + near[5]
        inverse = 1.0 / own
        drag = deposit[3, layer, :, :]
        slope = None
        for axis_no in range(3):
            mine = flow[axis_no, layer, :, :]
            moment = own * mine
            row = M_ROWS + axis_no * EDGE + layer
            summed = (
                moment_layer(axis_no, layer + 1) + moment_layer(axis_no, layer - 1)
                + row_up(moment, right[row : row + 1, :]) + row_down(moment, left[row : row + 1, :])
                + lane_up(moment) + lane_down(moment)
            )
            rate = VISCOSITY * (summed - mine * around) + (
                deposit[axis_no, layer, :, :] - drag * mine
            ) * inverse
            history_out[0, axis_no, layer, :, :] = rate
            history_out[1, axis_no, layer, :, :] = latest[axis_no, layer, :, :]
            trial = base[axis_no, layer, :, :] + (TIME_STEP * WEIGHT_NEW) * rate
            trial_out[axis_no, layer, :, :] = trial
            part = trial * (near[2 * axis_no] - near[2 * axis_no + 1])
            slope = part if axis_no == 0 else slope + part
            weighted = own * trial
            if axis_no == 0:
                scaled[layer, :, :] = weighted
            if axis_no == 1:
                slope = slope + row_up(weighted, 0.0) - row_down(weighted, 0.0)
                edge_out[0, layer : layer + 1, :] = weighted[0:1, :]
                edge_out[1, layer : layer + 1, :] = weighted[EDGE - 1 : EDGE, :]
            if axis_no == 2:
                slope = slope + lane_up(weighted) - lane_down(weighted)
        div_out[layer, :, :] = slope
    for layer in range(EDGE):
        total = div_out[layer, :, :]
        if layer < EDGE - 1:
            total = total + scaled[layer + 1, :, :]
        if layer > 0:
            total = total - scaled[layer - 1, :, :]
        div_out[layer, :, :] = total
        if layer < REACH:
            to_lower[layer, :, :] = total
        if layer >= EDGE - REACH:
            to_upper[layer - EDGE + REACH, :, :] = total
    for send, layer, start in ((to_lower, 0, 0), (to_upper, EDGE - 1, EDGE - REACH)):
        send[REACH, :, :] = scaled[layer, :, :]
        for side in range(2):
            send[REACH + 1, side * 8 : side * 8 + REACH, :] = edge_out[side, start : start + REACH, :]
            send[REACH + 1, side * 8 + REACH : side * 8 + 8, :] = jnp.zeros((8 - REACH, LANES), F32)


def pack_div_kernel(div, sent_lower, sent_upper, edge, lower, upper, wide_out, to_right, to_left):
    for layer in range(SPAN):
        if layer < REACH:
            value = lower[layer, :, :]
            if layer == REACH - 1:
                value = value + sent_lower[REACH, :, :]
        elif layer < REACH + EDGE:
            value = div[layer - REACH, :, :]
            if layer == REACH:
                value = value - lower[REACH, :, :]
            if layer == REACH + EDGE - 1:
                value = value + upper[REACH, :, :]
        else:
            value = upper[layer - REACH - EDGE, :, :]
            if layer == REACH + EDGE:
                value = value - sent_upper[REACH, :, :]
        wide_out[layer, :, :] = value
        row = layer * ROWS
        to_right[row : row + ROWS, :] = value[8:16, :]
        to_left[row : row + ROWS, :] = value[0:8, :]
    start = SPAN * ROWS
    for send, side in ((to_left, 0), (to_right, 1)):
        for layer in range(REACH):
            row = start + layer
            send[row : row + 1, :] = lower[REACH + 1, side * 8 + layer : side * 8 + layer + 1, :]
            row = start + REACH + EDGE + layer
            send[row : row + 1, :] = upper[REACH + 1, side * 8 + layer : side * 8 + layer + 1, :]
        for layer in range(EDGE):
            row = start + REACH + layer
            send[row : row + 1, :] = edge[side, layer : layer + 1, :]
        send[start + SPAN : start + 32, :] = jnp.zeros((32 - SPAN, LANES), F32)


def widen_kernel(press, void, lower, upper, left, right, void_wide, press_wide, factor):
    for number, own, wide in ((0, void, void_wide), (1, press, press_wide)):
        for layer in range(WIDE):
            row = (number * WIDE + layer) * ROWS
            wide[layer, 0:8, :] = left[row : row + ROWS, :]
            wide[layer, 24:32, :] = right[row : row + ROWS, :]
            if layer < HALO:
                wide[layer, 8:24, :] = lower[number * HALO + layer, :, :]
            elif layer < HALO + EDGE:
                wide[layer, 8:24, :] = own[layer - HALO, :, :]
            else:
                wide[layer, 8:24, :] = upper[number * HALO + layer - HALO - EDGE, :, :]
    factor[0, :, :] = jnp.zeros((32, LANES), F32)
    factor[WIDE - 1, :, :] = jnp.zeros((32, LANES), F32)
    for layer in range(1, WIDE - 1):
        value = void_wide[layer, :, :]
        around = (
            void_wide[layer - 1, :, :] + void_wide[layer + 1, :, :]
            + row_up(value, 0.0) + row_down(value, 0.0) + lane_up(value) + lane_down(value)
        )
        outside = around <= 0.0
        factor[layer, :, :] = jnp.where(outside, 0.0, RELAXATION / jnp.where(outside, 1.0, around))


def relax_kernel(
    trial, void_wide, press_wide, factor, wide_div, sent_left, sent_right, left, right,
    velocity_out, pressure_out, press, known, first, second,
):
    start = SPAN * ROWS
    for layer in range(SPAN):
        row = layer * ROWS
        edge = slice(start + layer, start + layer + 1)
        middle = wide_div[layer, :, :]
        west = left[row : row + ROWS, :]
        east = right[row : row + ROWS, :]
        block = jnp.concatenate([west, middle, east], axis=0)
        place = lax.broadcasted_iota(jnp.int32, (32, LANES), 0)
        block = block + jnp.where(place == 7, sent_left[edge, :], 0.0)
        block = block - jnp.where(place == 8, left[edge, :], 0.0)
        block = block + jnp.where(place == 23, right[edge, :], 0.0)
        block = block - jnp.where(place == 24, sent_right[edge, :], 0.0)
        known[layer + 1, :, :] = -2.0 * factor[layer + 1, :, :] * block
    for layer in range(WIDE):
        first[layer, :, :] = void_wide[layer, :, :] * press_wide[layer, :, :]
    for sweep in range(1, SWEEPS + 1):
        source, target = (first, second) if sweep % 2 == 1 else (second, first)
        before = press_wide if sweep == 1 else press
        for layer in range(sweep, WIDE - sweep):
            value = source[layer, :, :]
            around = (
                source[layer - 1, :, :] + source[layer + 1, :, :]
                + pltpu.roll(value, 31, 0) + pltpu.roll(value, 1, 0) + lane_up(value) + lane_down(value)
            )
            new = (
                (1.0 - RELAXATION) * before[layer, :, :] + known[layer, :, :]
                + factor[layer, :, :] * around
            )
            press[layer, :, :] = new
            if sweep < SWEEPS:
                target[layer, :, :] = void_wide[layer, :, :] * new
    half_step = 0.5 * TIME_STEP
    inner = slice(8, 24)
    for layer in range(HALO, HALO + EDGE):
        here = press[layer, :, :]
        void = void_wide[layer, :, :]
        centre = here[inner, :]
        pressure_out[layer - HALO, :, :] = centre

        def gradient(ahead, void_ahead, behind, void_behind):
            return void_ahead * (ahead - here) + void_behind * (here - behind)

        pieces = (
            gradient(press[layer + 1, :, :], void_wide[layer + 1, :, :], press[layer - 1, :, :], void_wide[layer - 1, :, :]),
            gradient(pltpu.roll(here, 31, 0), pltpu.roll(void, 31, 0), pltpu.roll(here, 1, 0), pltpu.roll(void, 1, 0)),
            gradient(lane_up(here), lane_up(void), lane_down(here), lane_down(void)),
        )
        for axis_no in range(3):
            velocity_out[axis_no, layer - HALO, :, :] = (
                trial[axis_no, layer - HALO, :, :] - half_step * pieces[axis_no][inner, :]
            )


def to_next(value, axis, periodic):
    count = lax.axis_size(axis)
    pairs = [(i, i + 1) for i in range(count - 1)] + ([(count - 1, 0)] if periodic else [])
    return lax.ppermute(value, axis, pairs)


def to_previous(value, axis, periodic):
    count = lax.axis_size(axis)
    pairs = [(i + 1, i) for i in range(count - 1)] + ([(0, count - 1)] if periodic else [])
    return lax.ppermute(value, axis, pairs)


def per_device(
    velocity, pressure, void_fraction, history, remap_list, parcel_records, parcel_owner, parcel_cells
):
    cells = pressure.shape
    codes = remap_list.transpose(1, 2, 0).reshape(-1, remap_list.shape[0])
    fields = (velocity, history, pressure, void_fraction)
    bricks = (FIELDS * 32, LANES)
    up, down = call(pack_kernel, [bricks, bricks], (codes,) + fields, smem=(0,))
    brick_low = to_next(up, "gz", True)
    brick_high = to_previous(down, "gz", True)
    (outgoing,) = call(
        dispatch_kernel,
        [(OWNERS, 8, CAP)],
        (parcel_records, parcel_owner.reshape(32, 128), parcel_cells.reshape(32, 128)),
        scratch=(pltpu.VMEM((PARCELS // BLOCK * OWNERS, BLOCK), BF16), pltpu.VMEM((512, 2 * CAP), F32)),
    )
    layers = (2 * HALO + 3, EDGE, LANES)
    flow, latest, base, press, void, up, down = call(
        remap_kernel,
        [(3,) + cells, (3,) + cells, (3,) + cells, cells, cells, layers, layers],
        (codes,) + fields + (brick_low, brick_high),
        smem=(0,),
    )
    state_low = to_next(up, "gz", True)
    state_high = to_previous(down, "gz", True)
    arrived = lax.all_to_all(outgoing, "gz", split_axis=0, concat_axis=0, tiled=True)
    rows = (2 * WIDE * ROWS + 3 * EDGE, LANES)
    right, left = call(pack_rows_kernel, [rows, rows], (flow, press, void, state_low, state_high))
    state_left = to_next(right, "gx", False)
    state_right = to_previous(left, "gx", False)
    (deposit,) = call(
        deposit_kernel, [(4,) + cells], (arrived,), scratch=(pltpu.VMEM((1024, 2 * LANES), F32),)
    )
    layers = (REACH + 2, EDGE, LANES)
    new_history, trial, div, up, down, edge = call(
        rate_kernel,
        [(2, 3) + cells, (3,) + cells, cells, layers, layers, (2, EDGE, LANES)],
        (flow, latest, base, void, state_low, state_high, state_left, state_right, deposit),
        scratch=(pltpu.VMEM(cells, F32),),
    )
    div_low = to_next(up, "gz", True)
    div_high = to_previous(down, "gz", True)
    wide = (WIDE, 32, LANES)
    void_wide, press_wide, factor = call(
        widen_kernel, [wide, wide, wide], (press, void, state_low, state_high, state_left, state_right)
    )
    rows = (SPAN * ROWS + 32, LANES)
    wide_div, right, left = call(
        pack_div_kernel,
        [(SPAN, EDGE, LANES), rows, rows],
        (div, down, up, edge, div_low, div_high),
    )
    div_left = to_next(right, "gx", False)
    div_right = to_previous(left, "gx", False)
    new_velocity, new_pressure = call(
        relax_kernel,
        [(3,) + cells, cells],
        (trial, void_wide, press_wide, factor, wide_div, left, right, div_left, div_right),
        scratch=(pltpu.VMEM(wide, F32), pltpu.VMEM(wide, F32), pltpu.VMEM(wide, F32), pltpu.VMEM(wide, F32)),
    )
    return new_velocity, new_pressure, new_history


def solution(mesh):
    return jax.shard_map(
        per_device,
        mesh=mesh,
        in_specs=(
            P(None, "gz", "gx", None),
            P("gz", "gx", None),
            P("gz", "gx", None),
            P(None, None, "gz", "gx", None),
            P(),
            P(None, ("gz", "gx")),
            P(("gz", "gx"), None),
            P(("gz", "gx")),
        ),
        out_specs=(P(None, "gz", "gx", None), P("gz", "gx", None), P(None, None, "gz", "gx", None)),
        check_vma=False,
    )
```

```python
import jax
import jax.numpy as jnp
from jax import lax
from jax.experimental import pallas as pl
from jax.experimental.pallas import tpu as pltpu
from jax.sharding import PartitionSpec as P

SWEEPS = 6
TIME_STEP = 0.25
VISCOSITY = 0.5
DRAG_SCALE = 0.5
RELAXATION = 0.8
WEIGHT_NEW = 23.0 / 12.0
WEIGHT_LAST = 16.0 / 12.0
WEIGHT_OLDER = 5.0 / 12.0

BRICK = 16
BRICKS = 8
EDGE = 16
LANES = 128
ROWS = 8
HALO = SWEEPS + 1
WIDE = HALO + EDGE + HALO
REACH = SWEEPS
SPAN = REACH + EDGE + REACH
FIELDS = 11
OWNERS = 64
CAP = 128
PARCELS = 4096
BLOCK = 256
STEP = 4
VMEM_LIMIT = 48 * 1024 * 1024

F32 = jnp.float32
BF16 = jnp.bfloat16


def call(kernel, outs, args, spaces=None, scratch=()):
    spaces = spaces or {}
    shapes = [out if isinstance(out, jax.ShapeDtypeStruct) else jax.ShapeDtypeStruct(out, F32) for out in outs]
    return pl.pallas_call(
        kernel,
        out_shape=shapes,
        in_specs=[
            pl.BlockSpec(memory_space=spaces.get(number, pltpu.VMEM)) for number in range(len(args))
        ],
        out_specs=[pl.BlockSpec(memory_space=pltpu.VMEM) for _ in outs],
        scratch_shapes=list(scratch),
        compiler_params=pltpu.CompilerParams(vmem_limit_bytes=VMEM_LIMIT),
    )(*args)


def lane_of():
    return lax.broadcasted_iota(jnp.int32, (ROWS, LANES), 1)


def take(block, index):
    return jnp.take_along_axis(block, index, axis=1, mode="promise_in_bounds")


def field_block(refs, field, tile):
    velocity, history, pressure, void = refs
    layer, half = tile // 2, tile % 2
    rows = slice(half * ROWS, (half + 1) * ROWS)
    if field < 3:
        return velocity[field, layer, rows, :]
    if field < 9:
        return history[(field - 3) // 3, field % 3, layer, rows, :]
    return (pressure if field == 9 else void)[layer, rows, :]


def pack_bricks(codes, refs, to_upper, to_lower, code_out):
    cycle = lax.axis_index("gz")
    line = lax.axis_index("gx")
    size = lax.axis_size("gz")
    upper = lax.rem(cycle + 1, size)
    lower = lax.rem(cycle + size - 1, size)
    slot_up = jnp.int32(0)
    slot_down = jnp.int32(0)
    lane = lane_of()
    group = lane // BRICK
    code_of = jnp.zeros((ROWS, LANES), jnp.int32)
    for brick in range(BRICKS):
        code = codes[line * BRICKS + brick, upper]
        slot_up = slot_up + jnp.where(code < BRICKS, code, 0)
        code = codes[line * BRICKS + brick, lower]
        slot_down = slot_down + jnp.where(code >= 2 * BRICKS, code - 2 * BRICKS, 0)
        code_of = jnp.where(group == brick, codes[line * BRICKS + brick, cycle], code_of)
    code_out[...] = code_of
    index_up = slot_up * BRICK + lane % BRICK
    index_down = slot_down * BRICK + lane % BRICK
    for field in range(FIELDS):
        for part in range(4):
            up = jnp.zeros((ROWS, LANES), F32)
            down = jnp.zeros((ROWS, LANES), F32)
            for place in range(8):
                block = field_block(refs, field, part * 8 + place)
                up = jnp.where(group == place, take(block, index_up), up)
                down = jnp.where(group == place, take(block, index_down), down)
            row = (field * 4 + part) * ROWS
            to_upper[row : row + ROWS, :] = up
            to_lower[row : row + ROWS, :] = down


def copied(sources, targets, arrivals):
    return [
        pltpu.make_async_copy(source, target, arrivals.at[number])
        for number, (source, target) in enumerate(zip(sources, targets))
    ]


def pack_kernel(*refs):
    sources, (to_upper, to_lower, code_out), held, arrivals = refs[:5], refs[5:8], refs[8:13], refs[13]
    copies = copied(sources, held, arrivals)
    for copy in copies:
        copy.start()
    for copy in copies:
        copy.wait()
    pack_bricks(held[0], held[1:], to_upper, to_lower, code_out)


def remapper(code_ref, refs, lower, upper):
    lane = lane_of()
    code_of = code_ref[...]
    from_lower = code_of < BRICKS
    from_upper = code_of >= 2 * BRICKS
    index_own = (code_of % BRICKS) * BRICK + lane % BRICK

    def moved(field, tile):
        part, place = tile // 8, tile % 8
        index_in = place * BRICK + lane % BRICK
        row = (field * 4 + part) * ROWS
        own = take(field_block(refs, field, tile), index_own)
        low = take(lower[row : row + ROWS, :], index_in)
        high = take(upper[row : row + ROWS, :], index_in)
        return jnp.where(from_lower, low, jnp.where(from_upper, high, own))

    return moved


def tile_at(tile):
    half = tile % 2
    return tile // 2, slice(half * ROWS, (half + 1) * ROWS)


def remap_first_kernel(
    codes, velocity, history, pressure, void, lower, upper, press_out, void_out, to_upper, to_lower
):
    moved = remapper(codes, (velocity, history, pressure, void), lower, upper)
    for tile in range(32):
        layer, rows = tile_at(tile)
        press, void_new = moved(9, tile), moved(10, tile)
        press_out[layer, rows, :] = press
        void_out[layer, rows, :] = void_new
        for send, edge in ((to_lower, 0), (to_upper, EDGE - 1)):
            if layer == edge:
                for axis_no in range(3):
                    send[2 * HALO + axis_no, rows, :] = void_new * moved(axis_no, tile)
        if layer < HALO:
            to_lower[layer, rows, :] = void_new
            to_lower[HALO + layer, rows, :] = press
        if layer >= EDGE - HALO:
            to_upper[layer - EDGE + HALO, rows, :] = void_new
            to_upper[2 * HALO + layer - EDGE, rows, :] = press


def remap_rest_kernel(
    codes, velocity, history, pressure, void, lower, upper, flow_out, latest_out, base_out
):
    moved = remapper(codes, (velocity, history, pressure, void), lower, upper)
    for tile in range(32):
        layer, rows = tile_at(tile)
        for axis_no in range(3):
            flow, latest, older = [moved(axis_no + kind, tile) for kind in (0, 3, 6)]
            flow_out[axis_no, layer, rows, :] = flow
            latest_out[axis_no, layer, rows, :] = latest
            base_out[axis_no, layer, rows, :] = flow + TIME_STEP * (
                WEIGHT_OLDER * older - WEIGHT_LAST * latest
            )


def pack_rows_kernel(flow, press, void, lower, upper, to_right, to_left):
    for send, rows, edge in ((to_right, slice(8, 16), EDGE - 1), (to_left, slice(0, 8), 0)):
        for number, own in ((0, void), (1, press)):
            start = number * WIDE * ROWS
            for layer in range(HALO):
                row = start + layer * ROWS
                send[row : row + ROWS, :] = lower[number * HALO + layer, rows, :]
                row = start + (HALO + EDGE + layer) * ROWS
                send[row : row + ROWS, :] = upper[number * HALO + layer, rows, :]
            for layer in range(EDGE):
                row = start + (HALO + layer) * ROWS
                send[row : row + ROWS, :] = own[layer, rows, :]
        for axis_no in range(3):
            row = 2 * WIDE * ROWS + axis_no * EDGE
            send[row : row + EDGE, :] = void[:, edge, :] * flow[axis_no, :, edge, :]


def split_two(value):
    high = value.astype(BF16)
    return high, (value - high.astype(F32)).astype(BF16)


NT = (((1,), (1,)), ((), ()))


def dispatch_kernel(records, owners, cells, out, shown, total):
    blocks = PARCELS // BLOCK
    owner_iota = lax.broadcasted_iota(jnp.int32, (OWNERS, BLOCK), 0)
    before = (
        lax.broadcasted_iota(jnp.int32, (BLOCK, BLOCK), 0)
        < lax.broadcasted_iota(jnp.int32, (BLOCK, BLOCK), 1)
    ).astype(F32).astype(BF16)

    def row_of(ref, block):
        return jnp.concatenate([ref[2 * block : 2 * block + 1, :], ref[2 * block + 1 : 2 * block + 2, :]], axis=1)

    for block in range(blocks):
        hit = (row_of(owners, block) == owner_iota).astype(F32)
        shown[block * OWNERS : (block + 1) * OWNERS, :] = hit.astype(BF16)
    earlier = lax.dot_general(
        shown[...], before, (((1,), (0,)), ((), ())), preferred_element_type=F32
    )
    base = jnp.zeros((OWNERS, 1), F32)
    row_iota = lax.broadcasted_iota(jnp.int32, (4, BLOCK), 0)
    key_iota = lax.broadcasted_iota(jnp.int32, (2 * CAP, BLOCK), 0)
    total[...] = jnp.zeros_like(total)
    for block in range(blocks):
        rows = slice(block * OWNERS, (block + 1) * OWNERS)
        hit = shown[rows, :].astype(F32)
        seen = earlier[block * OWNERS : (block + 1) * OWNERS, :]
        rank = jnp.sum(hit * (seen + base), axis=0, keepdims=True).astype(jnp.int32)
        base = base + seen[:, BLOCK - 1 : BLOCK] + hit[:, BLOCK - 1 : BLOCK]
        owner = row_of(owners, block)
        cell = row_of(cells, block)
        key = (owner // 32) * CAP + rank
        placed = (key == key_iota).astype(F32).astype(BF16)
        lanes = slice(block * BLOCK, (block + 1) * BLOCK)
        terms = jnp.zeros((4, BLOCK), F32)
        for size_class in range(4):
            state = records[4 * size_class : 4 * size_class + 4, lanes]
            coefficient = DRAG_SCALE * jnp.exp(state[3:4, :])
            terms = terms + coefficient * jnp.where(row_iota == 3, 1.0, state)
        depth, across, along = cell // 2048, (cell // LANES) % EDGE, cell % LANES
        major = (depth * 8 + across % 8).astype(F32)
        minor = ((across // 8) * LANES + along).astype(F32)
        blank2 = jnp.zeros((2, BLOCK), F32)
        blank4 = jnp.zeros((4, BLOCK), F32)
        coarse = terms.astype(BF16).astype(F32)
        values = jnp.concatenate(
            [coarse, major, minor, blank2, terms - coarse, blank4], axis=0
        ).astype(BF16)
        group = jnp.broadcast_to(owner % 32, (16, BLOCK)).astype(F32).astype(BF16)
        spread = jnp.concatenate(
            [jnp.where(group == jnp.asarray(number, BF16), values, jnp.zeros_like(values)) for number in range(32)],
            axis=0,
        )
        total[...] += lax.dot_general(spread, placed, NT, preferred_element_type=F32)
    for owner in range(OWNERS):
        row = (owner % 32) * 16
        lanes = slice((owner // 32) * CAP, (owner // 32 + 1) * CAP)
        out[owner, :, :] = total[row : row + 8, lanes] + total[row + 8 : row + 16, lanes]


def deposit_kernel(arrived, out, total, spread):
    iota_major = lax.broadcasted_iota(jnp.int32, (128, CAP), 0).astype(F32).astype(BF16)
    iota_minor = lax.broadcasted_iota(jnp.int32, (2 * LANES, CAP), 0).astype(F32).astype(BF16)
    zero = jnp.zeros((128, CAP), BF16)
    for start in range(0, OWNERS, STEP):
        placed = []
        for place in range(STEP):
            slots = arrived[start + place, :, :]
            lanes = slice(place * CAP, (place + 1) * CAP)
            here = jnp.broadcast_to(slots[4:5, :], (128, CAP)).astype(BF16) == iota_major
            for channel in range(4):
                value = slots[channel : channel + 1, :]
                coarse = value.astype(BF16).astype(F32)
                for part, piece in ((0, coarse), (1, value - coarse)):
                    row = (channel * 2 + part) * 128
                    spread[row : row + 128, lanes] = jnp.where(
                        here, jnp.broadcast_to(piece, (128, CAP)).astype(BF16), zero
                    )
            minor = jnp.broadcast_to(slots[5:6, :], (2 * LANES, CAP)).astype(BF16)
            placed.append(jnp.where(minor == iota_minor, jnp.ones_like(minor), jnp.zeros_like(minor)))
        summed = lax.dot_general(
            spread[...], jnp.concatenate(placed, axis=1), NT, preferred_element_type=F32
        )
        if start == 0:
            total[...] = summed
        else:
            total[...] += summed
    for channel in range(4):
        row = channel * 256
        for half in range(2):
            lanes = slice(half * LANES, (half + 1) * LANES)
            both = total[row : row + 128, lanes] + total[row + 128 : row + 256, lanes]
            out[channel, :, half * ROWS : (half + 1) * ROWS, :] = both.reshape(EDGE, ROWS, LANES)


def lane_up(value):
    lane = lax.broadcasted_iota(jnp.int32, value.shape, 1)
    return jnp.where(lane == LANES - 1, 0.0, pltpu.roll(value, LANES - 1, 1))


def lane_down(value):
    lane = lax.broadcasted_iota(jnp.int32, value.shape, 1)
    return jnp.where(lane == 0, 0.0, pltpu.roll(value, 1, 1))


def row_up(value, after):
    count = value.shape[0]
    row = lax.broadcasted_iota(jnp.int32, value.shape, 0)
    return jnp.where(row == count - 1, after, pltpu.roll(value, count - 1, 0))


def row_down(value, before):
    row = lax.broadcasted_iota(jnp.int32, value.shape, 0)
    return jnp.where(row == 0, before, pltpu.roll(value, 1, 0))


def has_neighbours():
    line = lax.axis_index("gx")
    return line > 0, line < lax.axis_size("gx") - 1


M_LOW = 2 * HALO
M_ROWS = 2 * WIDE * ROWS


def rate_kernel(
    flow, latest, base, void, lower, upper, left, right, deposit,
    history_out, trial_out, div_out, to_upper, to_lower, edge_out, scaled,
):
    def void_layer(layer):
        if layer < 0:
            return lower[HALO + layer, :, :]
        if layer >= EDGE:
            return upper[layer - EDGE, :, :]
        return void[layer, :, :]

    def moment_layer(axis_no, layer):
        if layer < 0:
            return lower[M_LOW + axis_no, :, :]
        if layer >= EDGE:
            return upper[M_LOW + axis_no, :, :]
        return void[layer, :, :] * flow[axis_no, layer, :, :]

    inside_left, inside_right = has_neighbours()
    for layer in range(EDGE):
        own = void[layer, :, :]
        row = (HALO + layer) * ROWS
        void_left = jnp.where(inside_left, left[row + ROWS - 1 : row + ROWS, :], 0.0)
        void_right = jnp.where(inside_right, right[row : row + 1, :], 0.0)
        near = (
            void_layer(layer + 1), void_layer(layer - 1),
            row_up(own, void_right), row_down(own, void_left),
            lane_up(own), lane_down(own),
        )
        around = near[0] + near[1] + near[2] + near[3] + near[4] + near[5]
        inverse = 1.0 / own
        drag = deposit[3, layer, :, :]
        slope = None
        for axis_no in range(3):
            mine = flow[axis_no, layer, :, :]
            moment = own * mine
            row = M_ROWS + axis_no * EDGE + layer
            summed = (
                moment_layer(axis_no, layer + 1) + moment_layer(axis_no, layer - 1)
                + row_up(moment, jnp.where(inside_right, right[row : row + 1, :], 0.0))
                + row_down(moment, jnp.where(inside_left, left[row : row + 1, :], 0.0))
                + lane_up(moment) + lane_down(moment)
            )
            rate = VISCOSITY * (summed - mine * around) + (
                deposit[axis_no, layer, :, :] - drag * mine
            ) * inverse
            history_out[0, axis_no, layer, :, :] = rate
            history_out[1, axis_no, layer, :, :] = latest[axis_no, layer, :, :]
            trial = base[axis_no, layer, :, :] + (TIME_STEP * WEIGHT_NEW) * rate
            trial_out[axis_no, layer, :, :] = trial
            part = trial * (near[2 * axis_no] - near[2 * axis_no + 1])
            slope = part if axis_no == 0 else slope + part
            weighted = own * trial
            if axis_no == 0:
                scaled[layer, :, :] = weighted
            if axis_no == 1:
                slope = slope + row_up(weighted, 0.0) - row_down(weighted, 0.0)
                edge_out[0, layer : layer + 1, :] = weighted[0:1, :]
                edge_out[1, layer : layer + 1, :] = weighted[EDGE - 1 : EDGE, :]
            if axis_no == 2:
                slope = slope + lane_up(weighted) - lane_down(weighted)
        div_out[layer, :, :] = slope
    for layer in range(EDGE):
        total = div_out[layer, :, :]
        if layer < EDGE - 1:
            total = total + scaled[layer + 1, :, :]
        if layer > 0:
            total = total - scaled[layer - 1, :, :]
        div_out[layer, :, :] = total
        if layer < REACH:
            to_lower[layer, :, :] = total
        if layer >= EDGE - REACH:
            to_upper[layer - EDGE + REACH, :, :] = total
    for send, layer, start in ((to_lower, 0, 0), (to_upper, EDGE - 1, EDGE - REACH)):
        send[REACH, :, :] = scaled[layer, :, :]
        for side in range(2):
            send[REACH + 1, side * 8 : side * 8 + REACH, :] = edge_out[side, start : start + REACH, :]
            send[REACH + 1, side * 8 + REACH : side * 8 + 8, :] = jnp.zeros((8 - REACH, LANES), F32)


def pack_div_kernel(div, sent_lower, sent_upper, edge, lower, upper, wide_out, to_right, to_left):
    for layer in range(SPAN):
        if layer < REACH:
            value = lower[layer, :, :]
            if layer == REACH - 1:
                value = value + sent_lower[REACH, :, :]
        elif layer < REACH + EDGE:
            value = div[layer - REACH, :, :]
            if layer == REACH:
                value = value - lower[REACH, :, :]
            if layer == REACH + EDGE - 1:
                value = value + upper[REACH, :, :]
        else:
            value = upper[layer - REACH - EDGE, :, :]
            if layer == REACH + EDGE:
                value = value - sent_upper[REACH, :, :]
        wide_out[layer, :, :] = value
        row = layer * ROWS
        to_right[row : row + ROWS, :] = value[8:16, :]
        to_left[row : row + ROWS, :] = value[0:8, :]
    start = SPAN * ROWS
    for send, side in ((to_left, 0), (to_right, 1)):
        for layer in range(REACH):
            row = start + layer
            send[row : row + 1, :] = lower[REACH + 1, side * 8 + layer : side * 8 + layer + 1, :]
            row = start + REACH + EDGE + layer
            send[row : row + 1, :] = upper[REACH + 1, side * 8 + layer : side * 8 + layer + 1, :]
        for layer in range(EDGE):
            row = start + REACH + layer
            send[row : row + 1, :] = edge[side, layer : layer + 1, :]
        send[start + SPAN : start + 32, :] = jnp.zeros((32 - SPAN, LANES), F32)


def widen_kernel(press, void, lower, upper, left, right, void_wide, press_wide, factor):
    inside_left, inside_right = has_neighbours()
    for number, own, wide in ((0, void, void_wide), (1, press, press_wide)):
        for layer in range(WIDE):
            row = (number * WIDE + layer) * ROWS
            wide[layer, 0:8, :] = jnp.where(inside_left, left[row : row + ROWS, :], 0.0)
            wide[layer, 24:32, :] = jnp.where(inside_right, right[row : row + ROWS, :], 0.0)
            if layer < HALO:
                wide[layer, 8:24, :] = lower[number * HALO + layer, :, :]
            elif layer < HALO + EDGE:
                wide[layer, 8:24, :] = own[layer - HALO, :, :]
            else:
                wide[layer, 8:24, :] = upper[number * HALO + layer - HALO - EDGE, :, :]
    factor[0, :, :] = jnp.zeros((32, LANES), F32)
    factor[WIDE - 1, :, :] = jnp.zeros((32, LANES), F32)
    for layer in range(1, WIDE - 1):
        value = void_wide[layer, :, :]
        around = (
            void_wide[layer - 1, :, :] + void_wide[layer + 1, :, :]
            + row_up(value, 0.0) + row_down(value, 0.0) + lane_up(value) + lane_down(value)
        )
        outside = around <= 0.0
        factor[layer, :, :] = jnp.where(outside, 0.0, RELAXATION / jnp.where(outside, 1.0, around))


def relax_kernel(
    trial, void_wide, press_wide, factor, wide_div, sent_left, sent_right, left, right,
    velocity_out, pressure_out, press, known, first, second,
):
    inside_left, inside_right = has_neighbours()
    start = SPAN * ROWS
    for layer in range(SPAN):
        row = layer * ROWS
        edge = slice(start + layer, start + layer + 1)
        middle = wide_div[layer, :, :]
        west = left[row : row + ROWS, :]
        east = right[row : row + ROWS, :]
        block = jnp.concatenate([west, middle, east], axis=0)
        place = lax.broadcasted_iota(jnp.int32, (32, LANES), 0)
        block = block + jnp.where(place == 7, sent_left[edge, :], 0.0)
        block = block - jnp.where((place == 8) & inside_left, left[edge, :], 0.0)
        block = block + jnp.where((place == 23) & inside_right, right[edge, :], 0.0)
        block = block - jnp.where(place == 24, sent_right[edge, :], 0.0)
        known[layer + 1, :, :] = -2.0 * factor[layer + 1, :, :] * block
    for layer in range(WIDE):
        first[layer, :, :] = void_wide[layer, :, :] * press_wide[layer, :, :]
    for sweep in range(1, SWEEPS + 1):
        source, target = (first, second) if sweep % 2 == 1 else (second, first)
        before = press_wide if sweep == 1 else press
        for layer in range(sweep, WIDE - sweep):
            value = source[layer, :, :]
            around = (
                source[layer - 1, :, :] + source[layer + 1, :, :]
                + pltpu.roll(value, 31, 0) + pltpu.roll(value, 1, 0) + lane_up(value) + lane_down(value)
            )
            new = (
                (1.0 - RELAXATION) * before[layer, :, :] + known[layer, :, :]
                + factor[layer, :, :] * around
            )
            press[layer, :, :] = new
            if sweep < SWEEPS:
                target[layer, :, :] = void_wide[layer, :, :] * new
    half_step = 0.5 * TIME_STEP
    inner = slice(8, 24)
    for layer in range(HALO, HALO + EDGE):
        here = press[layer, :, :]
        void = void_wide[layer, :, :]
        centre = here[inner, :]
        pressure_out[layer - HALO, :, :] = centre

        def gradient(ahead, void_ahead, behind, void_behind):
            return void_ahead * (ahead - here) + void_behind * (here - behind)

        pieces = (
            gradient(press[layer + 1, :, :], void_wide[layer + 1, :, :], press[layer - 1, :, :], void_wide[layer - 1, :, :]),
            gradient(pltpu.roll(here, 31, 0), pltpu.roll(void, 31, 0), pltpu.roll(here, 1, 0), pltpu.roll(void, 1, 0)),
            gradient(lane_up(here), lane_up(void), lane_down(here), lane_down(void)),
        )
        for axis_no in range(3):
            velocity_out[axis_no, layer - HALO, :, :] = (
                trial[axis_no, layer - HALO, :, :] - half_step * pieces[axis_no][inner, :]
            )


def shifted(value, axis, steps):
    count = lax.axis_size(axis)
    return lax.ppermute(value, axis, [(source, (source + steps) % count) for source in range(count)])


def per_device(
    velocity, pressure, void_fraction, history, remap_list, parcel_records, parcel_owner, parcel_cells
):
    cells = pressure.shape
    codes = remap_list.transpose(1, 2, 0).reshape(-1, remap_list.shape[0])
    fields = (velocity, history, pressure, void_fraction)
    bricks = (FIELDS * 32, LANES)
    inputs = (codes,) + fields
    up, down, code_of = call(
        pack_kernel,
        [bricks, bricks, jax.ShapeDtypeStruct((ROWS, LANES), jnp.int32)],
        tuple(pltpu.with_memory_space_constraint(value, pltpu.HBM) for value in inputs),
        spaces={number: pltpu.HBM for number in range(len(inputs))},
        scratch=[(pltpu.SMEM if value is codes else pltpu.VMEM)(value.shape, value.dtype) for value in inputs]
        + [pltpu.SemaphoreType.DMA((len(inputs),))],
    )
    (outgoing,) = call(
        dispatch_kernel,
        [(OWNERS, 8, CAP)],
        (parcel_records, parcel_owner.reshape(32, 128), parcel_cells.reshape(32, 128)),
        scratch=(pltpu.VMEM((PARCELS // BLOCK * OWNERS, BLOCK), BF16), pltpu.VMEM((512, 2 * CAP), F32)),
    )
    brick_low = shifted(up, "gz", 1)
    brick_high = shifted(down, "gz", -1)
    arrived = lax.all_to_all(outgoing, "gz", split_axis=0, concat_axis=0, tiled=True)
    layers = (2 * HALO + 3, EDGE, LANES)
    remap_inputs = (code_of,) + fields + (brick_low, brick_high)
    press, void, up, down = call(remap_first_kernel, [cells, cells, layers, layers], remap_inputs)
    state_low = shifted(up, "gz", 1)
    state_high = shifted(down, "gz", -1)
    flow, latest, base = call(remap_rest_kernel, [(3,) + cells] * 3, remap_inputs)
    (deposit,) = call(
        deposit_kernel,
        [(4,) + cells],
        (arrived,),
        scratch=(pltpu.VMEM((1024, 2 * LANES), F32), pltpu.VMEM((1024, STEP * CAP), BF16)),
    )
    rows = (2 * WIDE * ROWS + 3 * EDGE, LANES)
    right, left = call(
        pack_rows_kernel,
        [rows, rows],
        (flow, press, void, state_low, state_high),
    )
    state_left = shifted(right, "gx", 1)
    state_right = shifted(left, "gx", -1)
    new_history, trial, div, up, down, edge = call(
        rate_kernel,
        [(2, 3) + cells, (3,) + cells, cells, (REACH + 2,) + cells[1:], (REACH + 2,) + cells[1:], (2, EDGE, LANES)],
        (flow, latest, base, void, state_low, state_high, state_left, state_right, deposit),
        scratch=(pltpu.VMEM(cells, F32),),
    )
    div_low = shifted(up, "gz", 1)
    div_high = shifted(down, "gz", -1)
    wide = (WIDE, 2 * EDGE, LANES)
    void_wide, press_wide, factor = call(
        widen_kernel, [wide, wide, wide], (press, void, state_low, state_high, state_left, state_right)
    )
    rows = (SPAN * ROWS + 32, LANES)
    wide_div, right, left = call(
        pack_div_kernel, [(SPAN, EDGE, LANES), rows, rows], (div, down, up, edge, div_low, div_high)
    )
    div_left = shifted(right, "gx", 1)
    div_right = shifted(left, "gx", -1)
    new_velocity, new_pressure = call(
        relax_kernel,
        [(3,) + cells, cells],
        (trial, void_wide, press_wide, factor, wide_div, left, right, div_left, div_right),
        scratch=[pltpu.VMEM(wide, F32) for _ in range(4)],
    )
    return new_velocity, new_pressure, new_history


def solution(mesh):
    return jax.shard_map(
        per_device,
        mesh=mesh,
        in_specs=(
            P(None, "gz", "gx", None),
            P("gz", "gx", None),
            P("gz", "gx", None),
            P(None, None, "gz", "gx", None),
            P(),
            P(None, ("gz", "gx")),
            P(("gz", "gx"), None),
            P(("gz", "gx")),
        ),
        out_specs=(P(None, "gz", "gx", None), P("gz", "gx", None), P(None, None, "gz", "gx", None)),
        check_vma=False,
    )
```

```python
import jax
import jax.numpy as jnp
from jax import lax
from jax.experimental import pallas as pl
from jax.experimental.pallas import tpu as pltpu
from jax.sharding import PartitionSpec as P

SWEEPS = 6
TIME_STEP = 0.25
VISCOSITY = 0.5
DRAG_SCALE = 0.5
RELAXATION = 0.8
WEIGHT_NEW = 23.0 / 12.0
WEIGHT_LAST = 16.0 / 12.0
WEIGHT_OLDER = 5.0 / 12.0

BRICK = 16
BRICKS = 8
EDGE = 16
LANES = 128
ROWS = 8
HALO = SWEEPS + 1
WIDE = HALO + EDGE + HALO
REACH = SWEEPS
SPAN = REACH + EDGE + REACH
FIELDS = 11
OWNERS = 64
CAP = 128
PARCELS = 4096
BLOCK = 256
STEP = 4
VMEM_LIMIT = 16 * 1024 * 1024

F32 = jnp.float32
BF16 = jnp.bfloat16


def call(kernel, outs, args, spaces=None, scratch=(), far=(), aliases=None):
    spaces = spaces or {}
    shapes = [out if isinstance(out, jax.ShapeDtypeStruct) else jax.ShapeDtypeStruct(out, F32) for out in outs]
    shapes = [
        pltpu.HBM(shape.shape, shape.dtype) if number in far else shape for number, shape in enumerate(shapes)
    ]
    return pl.pallas_call(
        kernel,
        out_shape=shapes,
        in_specs=[
            pl.BlockSpec(memory_space=spaces.get(number, pltpu.VMEM)) for number in range(len(args))
        ],
        out_specs=[
            pl.BlockSpec(memory_space=pltpu.HBM if number in far else pltpu.VMEM) for number in range(len(outs))
        ],
        input_output_aliases=aliases or {},
        scratch_shapes=list(scratch),
        compiler_params=pltpu.CompilerParams(vmem_limit_bytes=VMEM_LIMIT),
    )(*args)


def lane_of():
    return lax.broadcasted_iota(jnp.int32, (ROWS, LANES), 1)


def take(block, index):
    return jnp.take_along_axis(block, index, axis=1, mode="promise_in_bounds")


def field_block(refs, field, tile):
    velocity, history, pressure, void = refs
    layer, half = tile // 2, tile % 2
    rows = slice(half * ROWS, (half + 1) * ROWS)
    if field < 3:
        return velocity[field, layer, rows, :]
    if field < 9:
        return history[(field - 3) // 3, field % 3, layer, rows, :]
    return (pressure if field == 9 else void)[layer, rows, :]


def pack_bricks(codes, refs, to_upper, to_lower, code_out, arrive):
    cycle = lax.axis_index("gz")
    line = lax.axis_index("gx")
    size = lax.axis_size("gz")
    upper = lax.rem(cycle + 1, size)
    lower = lax.rem(cycle + size - 1, size)
    slot_up = jnp.int32(0)
    slot_down = jnp.int32(0)
    lane = lane_of()
    group = lane // BRICK
    code_of = jnp.zeros((ROWS, LANES), jnp.int32)
    for brick in range(BRICKS):
        code = codes[line * BRICKS + brick, upper]
        slot_up = slot_up + jnp.where(code < BRICKS, code, 0)
        code = codes[line * BRICKS + brick, lower]
        slot_down = slot_down + jnp.where(code >= 2 * BRICKS, code - 2 * BRICKS, 0)
        code_of = jnp.where(group == brick, codes[line * BRICKS + brick, cycle], code_of)
    code_out[...] = code_of
    index_up = slot_up * BRICK + lane % BRICK
    index_down = slot_down * BRICK + lane % BRICK
    for field in (10, 9, 0, 1, 2, 3, 4, 5, 6, 7, 8):
        arrive(field)
        for part in range(4):
            up = jnp.zeros((ROWS, LANES), F32)
            down = jnp.zeros((ROWS, LANES), F32)
            for place in range(8):
                block = field_block(refs, field, part * 8 + place)
                up = jnp.where(group == place, take(block, index_up), up)
                down = jnp.where(group == place, take(block, index_down), down)
            row = (field * 4 + part) * ROWS
            to_upper[row : row + ROWS, :] = up
            to_lower[row : row + ROWS, :] = down


def copied(sources, targets, arrivals):
    return [
        pltpu.make_async_copy(source, target, arrivals.at[number])
        for number, (source, target) in enumerate(zip(sources, targets))
    ]


def pack_kernel(*refs):
    sources, (to_upper, to_lower, code_out), held, arrivals = refs[:5], refs[5:8], refs[8:13], refs[13]
    copies = copied(sources, held, arrivals)
    for number in (0, 4, 3, 1, 2):
        copies[number].start()
    copies[0].wait()

    def arrive(field):
        number = {10: 4, 9: 3, 0: 1, 3: 2}.get(field)
        if number is not None:
            copies[number].wait()

    pack_bricks(held[0], held[1:], to_upper, to_lower, code_out, arrive)


def remapper(code_ref, refs, lower, upper):
    lane = lane_of()
    code_of = code_ref[...]
    from_lower = code_of < BRICKS
    from_upper = code_of >= 2 * BRICKS
    index_own = (code_of % BRICKS) * BRICK + lane % BRICK

    def moved(field, tile):
        part, place = tile // 8, tile % 8
        index_in = place * BRICK + lane % BRICK
        row = (field * 4 + part) * ROWS
        own = take(field_block(refs, field, tile), index_own)
        low = take(lower[row : row + ROWS, :], index_in)
        high = take(upper[row : row + ROWS, :], index_in)
        return jnp.where(from_lower, low, jnp.where(from_upper, high, own))

    return moved


def tile_at(tile):
    half = tile % 2
    return tile // 2, slice(half * ROWS, (half + 1) * ROWS)


def remap_first_kernel(
    codes, velocity, history, pressure, void, lower, upper, press_out, void_out, to_upper, to_lower
):
    moved = remapper(codes, (velocity, history, pressure, void), lower, upper)
    for tile in range(32):
        layer, rows = tile_at(tile)
        press, void_new = moved(9, tile), moved(10, tile)
        press_out[layer, rows, :] = press
        void_out[layer, rows, :] = void_new
        for send, edge in ((to_lower, 0), (to_upper, EDGE - 1)):
            if layer == edge:
                for axis_no in range(3):
                    send[2 * HALO + axis_no, rows, :] = void_new * moved(axis_no, tile)
        if layer < HALO:
            to_lower[layer, rows, :] = void_new
            to_lower[HALO + layer, rows, :] = press
        if layer >= EDGE - HALO:
            to_upper[layer - EDGE + HALO, rows, :] = void_new
            to_upper[2 * HALO + layer - EDGE, rows, :] = press


def remap_rest_kernel(
    codes, velocity, history, pressure, void, lower, upper, flow_out, base_far, latest_far,
    base_out, latest_out, leaving,
):
    moved = remapper(codes, (velocity, history, pressure, void), lower, upper)
    copies = []
    for tile in range(32):
        layer, rows = tile_at(tile)
        for axis_no in range(3):
            flow, latest, older = [moved(axis_no + kind, tile) for kind in (0, 3, 6)]
            flow_out[axis_no, layer, rows, :] = flow
            latest_out[axis_no, layer, rows, :] = latest
            base_out[axis_no, layer, rows, :] = flow + TIME_STEP * (
                WEIGHT_OLDER * older - WEIGHT_LAST * latest
            )
        if tile % 8 == 7:
            part = pl.ds(tile // 8 * 4, 4)
            for source, target in ((base_out, base_far), (latest_out, latest_far)):
                copies.append(
                    pltpu.make_async_copy(source.at[:, part], target.at[:, part], leaving.at[len(copies)])
                )
                copies[-1].start()
    for copy in copies:
        copy.wait()


def pack_rows_kernel(flow, press, void, lower, upper, to_right, to_left):
    for send, rows, edge in ((to_right, slice(8, 16), EDGE - 1), (to_left, slice(0, 8), 0)):
        for number, own in ((0, void), (1, press)):
            start = number * WIDE * ROWS
            for layer in range(HALO):
                row = start + layer * ROWS
                send[row : row + ROWS, :] = lower[number * HALO + layer, rows, :]
                row = start + (HALO + EDGE + layer) * ROWS
                send[row : row + ROWS, :] = upper[number * HALO + layer, rows, :]
            for layer in range(EDGE):
                row = start + (HALO + layer) * ROWS
                send[row : row + ROWS, :] = own[layer, rows, :]
        for axis_no in range(3):
            row = 2 * WIDE * ROWS + axis_no * EDGE
            send[row : row + EDGE, :] = void[:, edge, :] * flow[axis_no, :, edge, :]


def split_two(value):
    high = value.astype(BF16)
    return high, (value - high.astype(F32)).astype(BF16)


NT = (((1,), (1,)), ((), ()))


def dispatch_kernel(records, owners, cells, out, shown, total):
    blocks = PARCELS // BLOCK
    owner_iota = lax.broadcasted_iota(jnp.int32, (OWNERS, BLOCK), 0)
    before = (
        lax.broadcasted_iota(jnp.int32, (BLOCK, BLOCK), 0)
        < lax.broadcasted_iota(jnp.int32, (BLOCK, BLOCK), 1)
    ).astype(F32).astype(BF16)

    def row_of(ref, block):
        return jnp.concatenate([ref[2 * block : 2 * block + 1, :], ref[2 * block + 1 : 2 * block + 2, :]], axis=1)

    for block in range(blocks):
        hit = (row_of(owners, block) == owner_iota).astype(F32)
        shown[block * OWNERS : (block + 1) * OWNERS, :] = hit.astype(BF16)
    earlier = lax.dot_general(
        shown[...], before, (((1,), (0,)), ((), ())), preferred_element_type=F32
    )
    base = jnp.zeros((OWNERS, 1), F32)
    row_iota = lax.broadcasted_iota(jnp.int32, (4, BLOCK), 0)
    key_iota = lax.broadcasted_iota(jnp.int32, (2 * CAP, BLOCK), 0)
    total[...] = jnp.zeros_like(total)
    for block in range(blocks):
        rows = slice(block * OWNERS, (block + 1) * OWNERS)
        hit = shown[rows, :].astype(F32)
        seen = earlier[block * OWNERS : (block + 1) * OWNERS, :]
        rank = jnp.sum(hit * (seen + base), axis=0, keepdims=True).astype(jnp.int32)
        base = base + seen[:, BLOCK - 1 : BLOCK] + hit[:, BLOCK - 1 : BLOCK]
        owner = row_of(owners, block)
        cell = row_of(cells, block)
        key = (owner // 32) * CAP + rank
        placed = (key == key_iota).astype(F32).astype(BF16)
        lanes = slice(block * BLOCK, (block + 1) * BLOCK)
        terms = jnp.zeros((4, BLOCK), F32)
        for size_class in range(4):
            state = records[4 * size_class : 4 * size_class + 4, lanes]
            coefficient = DRAG_SCALE * jnp.exp(state[3:4, :])
            terms = terms + coefficient * jnp.where(row_iota == 3, 1.0, state)
        depth, across, along = cell // 2048, (cell // LANES) % EDGE, cell % LANES
        major = (depth * 8 + across % 8).astype(F32)
        minor = ((across // 8) * LANES + along).astype(F32)
        blank2 = jnp.zeros((2, BLOCK), F32)
        blank4 = jnp.zeros((4, BLOCK), F32)
        coarse = terms.astype(BF16).astype(F32)
        values = jnp.concatenate(
            [coarse, major, minor, blank2, terms - coarse, blank4], axis=0
        ).astype(BF16)
        group = jnp.broadcast_to(owner % 32, (16, BLOCK)).astype(F32).astype(BF16)
        spread = jnp.concatenate(
            [jnp.where(group == jnp.asarray(number, BF16), values, jnp.zeros_like(values)) for number in range(32)],
            axis=0,
        )
        total[...] += lax.dot_general(spread, placed, NT, preferred_element_type=F32)
    for owner in range(OWNERS):
        row = (owner % 32) * 16
        lanes = slice((owner // 32) * CAP, (owner // 32 + 1) * CAP)
        out[owner, :, :] = total[row : row + 8, lanes] + total[row + 8 : row + 16, lanes]


def add_slots(arrived, sources, total, spread):
    iota_major = lax.broadcasted_iota(jnp.int32, (128, CAP), 0).astype(F32).astype(BF16)
    iota_minor = lax.broadcasted_iota(jnp.int32, (2 * LANES, CAP), 0).astype(F32).astype(BF16)
    zero = jnp.zeros((128, CAP), BF16)
    for start in sources:
        placed = []
        for place in range(STEP):
            slots = arrived[start + place, :, :]
            lanes = slice(place * CAP, (place + 1) * CAP)
            here = jnp.broadcast_to(slots[4:5, :], (128, CAP)).astype(BF16) == iota_major
            for channel in range(4):
                value = slots[channel : channel + 1, :]
                coarse = value.astype(BF16).astype(F32)
                for part, piece in ((0, coarse), (1, value - coarse)):
                    row = (channel * 2 + part) * 128
                    spread[row : row + 128, lanes] = jnp.where(
                        here, jnp.broadcast_to(piece, (128, CAP)).astype(BF16), zero
                    )
            minor = jnp.broadcast_to(slots[5:6, :], (2 * LANES, CAP)).astype(BF16)
            placed.append(jnp.where(minor == iota_minor, jnp.ones_like(minor), jnp.zeros_like(minor)))
        summed = lax.dot_general(
            spread[...], jnp.concatenate(placed, axis=1), NT, preferred_element_type=F32
        )
        if start == 0:
            total[...] = summed
        else:
            total[...] += summed


def deposit_kernel(arrived, out, total, spread):
    add_slots(arrived, range(0, OWNERS, STEP), total, spread)
    for channel in range(4):
        row = channel * 256
        for half in range(2):
            lanes = slice(half * LANES, (half + 1) * LANES)
            both = total[row : row + 128, lanes] + total[row + 128 : row + 256, lanes]
            out[channel, :, half * ROWS : (half + 1) * ROWS, :] = both.reshape(EDGE, ROWS, LANES)


def lane_up(value):
    lane = lax.broadcasted_iota(jnp.int32, value.shape, 1)
    return jnp.where(lane == LANES - 1, 0.0, pltpu.roll(value, LANES - 1, 1))


def lane_down(value):
    lane = lax.broadcasted_iota(jnp.int32, value.shape, 1)
    return jnp.where(lane == 0, 0.0, pltpu.roll(value, 1, 1))


def row_up(value, after):
    count = value.shape[0]
    row = lax.broadcasted_iota(jnp.int32, value.shape, 0)
    return jnp.where(row == count - 1, after, pltpu.roll(value, count - 1, 0))


def row_down(value, before):
    row = lax.broadcasted_iota(jnp.int32, value.shape, 0)
    return jnp.where(row == 0, before, pltpu.roll(value, 1, 0))


def has_neighbours():
    line = lax.axis_index("gx")
    return line > 0, line < lax.axis_size("gx") - 1


M_LOW = 2 * HALO
M_ROWS = 2 * WIDE * ROWS


def rate_kernel(
    flow, latest, base, void, lower, upper, left, right, deposit,
    history_out, trial_out, div_out, to_upper, to_lower, edge_out, scaled, arrival,
):
    last = pltpu.make_async_copy(latest, history_out.at[1], arrival)
    last.start()
    def void_layer(layer):
        if layer < 0:
            return lower[HALO + layer, :, :]
        if layer >= EDGE:
            return upper[layer - EDGE, :, :]
        return void[layer, :, :]

    def moment_layer(axis_no, layer):
        if layer < 0:
            return lower[M_LOW + axis_no, :, :]
        if layer >= EDGE:
            return upper[M_LOW + axis_no, :, :]
        return void[layer, :, :] * flow[axis_no, layer, :, :]

    inside_left, inside_right = has_neighbours()
    for layer in range(EDGE):
        own = void[layer, :, :]
        row = (HALO + layer) * ROWS
        void_left = jnp.where(inside_left, left[row + ROWS - 1 : row + ROWS, :], 0.0)
        void_right = jnp.where(inside_right, right[row : row + 1, :], 0.0)
        near = (
            void_layer(layer + 1), void_layer(layer - 1),
            row_up(own, void_right), row_down(own, void_left),
            lane_up(own), lane_down(own),
        )
        around = near[0] + near[1] + near[2] + near[3] + near[4] + near[5]
        inverse = 1.0 / own
        drag = deposit[3, layer, :, :]
        slope = None
        for axis_no in range(3):
            mine = flow[axis_no, layer, :, :]
            moment = own * mine
            row = M_ROWS + axis_no * EDGE + layer
            summed = (
                moment_layer(axis_no, layer + 1) + moment_layer(axis_no, layer - 1)
                + row_up(moment, jnp.where(inside_right, right[row : row + 1, :], 0.0))
                + row_down(moment, jnp.where(inside_left, left[row : row + 1, :], 0.0))
                + lane_up(moment) + lane_down(moment)
            )
            rate = VISCOSITY * (summed - mine * around) + (
                deposit[axis_no, layer, :, :] - drag * mine
            ) * inverse
            history_out[0, axis_no, layer, :, :] = rate
            trial = base[axis_no, layer, :, :] + (TIME_STEP * WEIGHT_NEW) * rate
            trial_out[axis_no, layer, :, :] = trial
            part = trial * (near[2 * axis_no] - near[2 * axis_no + 1])
            slope = part if axis_no == 0 else slope + part
            weighted = own * trial
            if axis_no == 0:
                scaled[layer, :, :] = weighted
            if axis_no == 1:
                slope = slope + row_up(weighted, 0.0) - row_down(weighted, 0.0)
                edge_out[0, layer : layer + 1, :] = weighted[0:1, :]
                edge_out[1, layer : layer + 1, :] = weighted[EDGE - 1 : EDGE, :]
            if axis_no == 2:
                slope = slope + lane_up(weighted) - lane_down(weighted)
        div_out[layer, :, :] = slope
    for layer in range(EDGE):
        total = div_out[layer, :, :]
        if layer < EDGE - 1:
            total = total + scaled[layer + 1, :, :]
        if layer > 0:
            total = total - scaled[layer - 1, :, :]
        div_out[layer, :, :] = total
        if layer < REACH:
            to_lower[layer, :, :] = total
        if layer >= EDGE - REACH:
            to_upper[layer - EDGE + REACH, :, :] = total
    for send, layer, start in ((to_lower, 0, 0), (to_upper, EDGE - 1, EDGE - REACH)):
        send[REACH, :, :] = scaled[layer, :, :]
        for side in range(2):
            send[REACH + 1, side * 8 : side * 8 + REACH, :] = edge_out[side, start : start + REACH, :]
            send[REACH + 1, side * 8 + REACH : side * 8 + 8, :] = jnp.zeros((8 - REACH, LANES), F32)
    last.wait()


def pack_div_kernel(div, sent_lower, sent_upper, edge, lower, upper, wide_out, to_right, to_left):
    for layer in range(SPAN):
        if layer < REACH:
            value = lower[layer, :, :]
            if layer == REACH - 1:
                value = value + sent_lower[REACH, :, :]
        elif layer < REACH + EDGE:
            value = div[layer - REACH, :, :]
            if layer == REACH:
                value = value - lower[REACH, :, :]
            if layer == REACH + EDGE - 1:
                value = value + upper[REACH, :, :]
        else:
            value = upper[layer - REACH - EDGE, :, :]
            if layer == REACH + EDGE:
                value = value - sent_upper[REACH, :, :]
        wide_out[layer, :, :] = value
        row = layer * ROWS
        to_right[row : row + ROWS, :] = value[8:16, :]
        to_left[row : row + ROWS, :] = value[0:8, :]
    start = SPAN * ROWS
    for send, side in ((to_left, 0), (to_right, 1)):
        for layer in range(REACH):
            row = start + layer
            send[row : row + 1, :] = lower[REACH + 1, side * 8 + layer : side * 8 + layer + 1, :]
            row = start + REACH + EDGE + layer
            send[row : row + 1, :] = upper[REACH + 1, side * 8 + layer : side * 8 + layer + 1, :]
        for layer in range(EDGE):
            row = start + REACH + layer
            send[row : row + 1, :] = edge[side, layer : layer + 1, :]
        send[start + SPAN : start + 32, :] = jnp.zeros((32 - SPAN, LANES), F32)


def widen_kernel(press, void, lower, upper, left, right, void_wide, press_wide, factor):
    inside_left, inside_right = has_neighbours()
    for number, own, wide in ((0, void, void_wide), (1, press, press_wide)):
        for layer in range(WIDE):
            row = (number * WIDE + layer) * ROWS
            wide[layer, 0:8, :] = jnp.where(inside_left, left[row : row + ROWS, :], 0.0)
            wide[layer, 24:32, :] = jnp.where(inside_right, right[row : row + ROWS, :], 0.0)
            if layer < HALO:
                wide[layer, 8:24, :] = lower[number * HALO + layer, :, :]
            elif layer < HALO + EDGE:
                wide[layer, 8:24, :] = own[layer - HALO, :, :]
            else:
                wide[layer, 8:24, :] = upper[number * HALO + layer - HALO - EDGE, :, :]
    factor[0, :, :] = jnp.zeros((32, LANES), F32)
    factor[WIDE - 1, :, :] = jnp.zeros((32, LANES), F32)
    for layer in range(1, WIDE - 1):
        value = void_wide[layer, :, :]
        around = (
            void_wide[layer - 1, :, :] + void_wide[layer + 1, :, :]
            + row_up(value, 0.0) + row_down(value, 0.0) + lane_up(value) + lane_down(value)
        )
        outside = around <= 0.0
        factor[layer, :, :] = jnp.where(outside, 0.0, RELAXATION / jnp.where(outside, 1.0, around))


def relax_kernel(
    trial, void_wide, press_wide, factor, wide_div, sent_left, sent_right, left, right,
    velocity_out, pressure_out, press, known, first, second,
):
    inside_left, inside_right = has_neighbours()
    start = SPAN * ROWS
    for layer in range(SPAN):
        row = layer * ROWS
        edge = slice(start + layer, start + layer + 1)
        middle = wide_div[layer, :, :]
        west = left[row : row + ROWS, :]
        east = right[row : row + ROWS, :]
        block = jnp.concatenate([west, middle, east], axis=0)
        place = lax.broadcasted_iota(jnp.int32, (32, LANES), 0)
        block = block + jnp.where(place == 7, sent_left[edge, :], 0.0)
        block = block - jnp.where((place == 8) & inside_left, left[edge, :], 0.0)
        block = block + jnp.where((place == 23) & inside_right, right[edge, :], 0.0)
        block = block - jnp.where(place == 24, sent_right[edge, :], 0.0)
        known[layer + 1, :, :] = -2.0 * factor[layer + 1, :, :] * block
    for layer in range(WIDE):
        first[layer, :, :] = void_wide[layer, :, :] * press_wide[layer, :, :]
    for sweep in range(1, SWEEPS + 1):
        source, target = (first, second) if sweep % 2 == 1 else (second, first)
        before = press_wide if sweep == 1 else press
        for layer in range(sweep, WIDE - sweep):
            value = source[layer, :, :]
            around = (
                source[layer - 1, :, :] + source[layer + 1, :, :]
                + pltpu.roll(value, 31, 0) + pltpu.roll(value, 1, 0) + lane_up(value) + lane_down(value)
            )
            new = (
                (1.0 - RELAXATION) * before[layer, :, :] + known[layer, :, :]
                + factor[layer, :, :] * around
            )
            press[layer, :, :] = new
            if sweep < SWEEPS:
                target[layer, :, :] = void_wide[layer, :, :] * new
    half_step = 0.5 * TIME_STEP
    inner = slice(8, 24)
    for layer in range(HALO, HALO + EDGE):
        here = press[layer, :, :]
        void = void_wide[layer, :, :]
        centre = here[inner, :]
        pressure_out[layer - HALO, :, :] = centre

        def gradient(ahead, void_ahead, behind, void_behind):
            return void_ahead * (ahead - here) + void_behind * (here - behind)

        pieces = (
            gradient(press[layer + 1, :, :], void_wide[layer + 1, :, :], press[layer - 1, :, :], void_wide[layer - 1, :, :]),
            gradient(pltpu.roll(here, 31, 0), pltpu.roll(void, 31, 0), pltpu.roll(here, 1, 0), pltpu.roll(void, 1, 0)),
            gradient(lane_up(here), lane_up(void), lane_down(here), lane_down(void)),
        )
        for axis_no in range(3):
            velocity_out[axis_no, layer - HALO, :, :] = (
                trial[axis_no, layer - HALO, :, :] - half_step * pieces[axis_no][inner, :]
            )


def shifted(value, axis, steps):
    count = lax.axis_size(axis)
    return lax.ppermute(value, axis, [(source, (source + steps) % count) for source in range(count)])


def per_device(
    velocity, pressure, void_fraction, history, remap_list, parcel_records, parcel_owner, parcel_cells
):
    cells = pressure.shape
    codes = remap_list.transpose(1, 2, 0).reshape(-1, remap_list.shape[0])
    fields = (velocity, history, pressure, void_fraction)
    bricks = (FIELDS * 32, LANES)
    inputs = (codes,) + fields
    up, down, code_of = call(
        pack_kernel,
        [bricks, bricks, jax.ShapeDtypeStruct((ROWS, LANES), jnp.int32)],
        tuple(pltpu.with_memory_space_constraint(value, pltpu.HBM) for value in inputs),
        spaces={number: pltpu.HBM for number in range(len(inputs))},
        scratch=[(pltpu.SMEM if value is codes else pltpu.VMEM)(value.shape, value.dtype) for value in inputs]
        + [pltpu.SemaphoreType.DMA((len(inputs),))],
    )
    (outgoing,) = call(
        dispatch_kernel,
        [(OWNERS, 8, CAP)],
        (parcel_records, parcel_owner.reshape(32, 128), parcel_cells.reshape(32, 128)),
        scratch=(pltpu.VMEM((PARCELS // BLOCK * OWNERS, BLOCK), BF16), pltpu.VMEM((512, 2 * CAP), F32)),
    )
    brick_low = shifted(up, "gz", 1)
    brick_high = shifted(down, "gz", -1)
    arrived = lax.all_to_all(outgoing, "gz", split_axis=0, concat_axis=0, tiled=True)
    layers = (2 * HALO + 3, EDGE, LANES)
    remap_inputs = (code_of,) + fields + (brick_low, brick_high)
    press, void, up, down = call(remap_first_kernel, [cells, cells, layers, layers], remap_inputs)
    state_low = shifted(up, "gz", 1)
    state_high = shifted(down, "gz", -1)
    flow, base, latest = call(
        remap_rest_kernel,
        [(3,) + cells] * 3,
        remap_inputs,
        scratch=[pltpu.VMEM((3,) + cells, F32)] * 2 + [pltpu.SemaphoreType.DMA((8,))],
        far=(1, 2),
    )
    sums = (1024, 2 * LANES)
    spread = pltpu.VMEM((1024, STEP * CAP), BF16)
    rows = (2 * WIDE * ROWS + 3 * EDGE, LANES)
    right, left = call(
        pack_rows_kernel,
        [rows, rows],
        (flow, press, void, state_low, state_high),
    )
    (deposit,) = call(
        deposit_kernel, [(4,) + cells], (arrived,), scratch=(pltpu.VMEM(sums, F32), spread)
    )
    state_left = shifted(right, "gx", 1)
    state_right = shifted(left, "gx", -1)
    latest = pltpu.with_memory_space_constraint(latest, pltpu.HBM)
    new_history, trial, div, up, down, edge = call(
        rate_kernel,
        [(2, 3) + cells, (3,) + cells, cells, (REACH + 2,) + cells[1:], (REACH + 2,) + cells[1:], (2, EDGE, LANES)],
        (flow, latest, base, void, state_low, state_high, state_left, state_right, deposit),
        spaces={1: pltpu.HBM},
        scratch=(pltpu.VMEM(cells, F32), pltpu.SemaphoreType.DMA(())),
    )
    div_low = shifted(up, "gz", 1)
    div_high = shifted(down, "gz", -1)
    wide = (WIDE, 2 * EDGE, LANES)
    void_wide, press_wide, factor = call(
        widen_kernel, [wide, wide, wide], (press, void, state_low, state_high, state_left, state_right)
    )
    rows = (SPAN * ROWS + 32, LANES)
    wide_div, right, left = call(
        pack_div_kernel, [(SPAN, EDGE, LANES), rows, rows], (div, down, up, edge, div_low, div_high)
    )
    div_left = shifted(right, "gx", 1)
    div_right = shifted(left, "gx", -1)
    new_velocity, new_pressure = call(
        relax_kernel,
        [(3,) + cells, cells],
        (trial, void_wide, press_wide, factor, wide_div, left, right, div_left, div_right),
        scratch=[pltpu.VMEM(wide, F32) for _ in range(4)],
    )
    return new_velocity, new_pressure, new_history


def solution(mesh):
    return jax.shard_map(
        per_device,
        mesh=mesh,
        in_specs=(
            P(None, "gz", "gx", None),
            P("gz", "gx", None),
            P("gz", "gx", None),
            P(None, None, "gz", "gx", None),
            P(),
            P(None, ("gz", "gx")),
            P(("gz", "gx"), None),
            P(("gz", "gx")),
        ),
        out_specs=(P(None, "gz", "gx", None), P("gz", "gx", None), P(None, None, "gz", "gx", None)),
        check_vma=False,
    )
```

```python
import jax
import jax.numpy as jnp
from jax import lax
from jax.experimental import pallas as pl
from jax.experimental.pallas import tpu as pltpu
from jax.sharding import PartitionSpec as P

SWEEPS = 6
TIME_STEP = 0.25
VISCOSITY = 0.5
DRAG_SCALE = 0.5
RELAXATION = 0.8
WEIGHT_NEW = 23.0 / 12.0
WEIGHT_LAST = 16.0 / 12.0
WEIGHT_OLDER = 5.0 / 12.0

BRICK = 16
BRICKS = 8
EDGE = 16
LANES = 128
ROWS = 8
HALO = SWEEPS + 1
WIDE = HALO + EDGE + HALO
REACH = SWEEPS
SPAN = REACH + EDGE + REACH
FIELDS = 11
OWNERS = 64
CAP = 128
PARCELS = 4096
BLOCK = 256
STEP = 4
VMEM_LIMIT = 16 * 1024 * 1024

F32 = jnp.float32
BF16 = jnp.bfloat16


def call(kernel, outs, args, spaces=None, scratch=(), far=(), aliases=None):
    spaces = spaces or {}
    shapes = [out if isinstance(out, jax.ShapeDtypeStruct) else jax.ShapeDtypeStruct(out, F32) for out in outs]
    shapes = [
        pltpu.HBM(shape.shape, shape.dtype) if number in far else shape for number, shape in enumerate(shapes)
    ]
    return pl.pallas_call(
        kernel,
        out_shape=shapes,
        in_specs=[
            pl.BlockSpec(memory_space=spaces.get(number, pltpu.VMEM)) for number in range(len(args))
        ],
        out_specs=[
            pl.BlockSpec(memory_space=pltpu.HBM if number in far else pltpu.VMEM) for number in range(len(outs))
        ],
        input_output_aliases=aliases or {},
        scratch_shapes=list(scratch),
        compiler_params=pltpu.CompilerParams(vmem_limit_bytes=VMEM_LIMIT),
    )(*args)


def lane_of():
    return lax.broadcasted_iota(jnp.int32, (ROWS, LANES), 1)


def take(block, index):
    return jnp.take_along_axis(block, index, axis=1, mode="promise_in_bounds")


def field_block(refs, field, tile):
    velocity, history, pressure, void = refs
    layer, half = tile // 2, tile % 2
    rows = slice(half * ROWS, (half + 1) * ROWS)
    if field < 3:
        return velocity[field, layer, rows, :]
    if field < 9:
        return history[(field - 3) // 3, field % 3, layer, rows, :]
    return (pressure if field == 9 else void)[layer, rows, :]


def pack_bricks(codes, refs, to_upper, to_lower, code_out, arrive):
    cycle = lax.axis_index("gz")
    line = lax.axis_index("gx")
    size = lax.axis_size("gz")
    upper = lax.rem(cycle + 1, size)
    lower = lax.rem(cycle + size - 1, size)
    slot_up = jnp.int32(0)
    slot_down = jnp.int32(0)
    lane = lane_of()
    group = lane // BRICK
    code_of = jnp.zeros((ROWS, LANES), jnp.int32)
    for brick in range(BRICKS):
        code = codes[line * BRICKS + brick, upper]
        slot_up = slot_up + jnp.where(code < BRICKS, code, 0)
        code = codes[line * BRICKS + brick, lower]
        slot_down = slot_down + jnp.where(code >= 2 * BRICKS, code - 2 * BRICKS, 0)
        code_of = jnp.where(group == brick, codes[line * BRICKS + brick, cycle], code_of)
    code_out[...] = code_of
    index_up = slot_up * BRICK + lane % BRICK
    index_down = slot_down * BRICK + lane % BRICK
    for field in (10, 9, 0, 1, 2, 3, 4, 5, 6, 7, 8):
        arrive(field)
        for part in range(4):
            up = jnp.zeros((ROWS, LANES), F32)
            down = jnp.zeros((ROWS, LANES), F32)
            for place in range(8):
                block = field_block(refs, field, part * 8 + place)
                up = jnp.where(group == place, take(block, index_up), up)
                down = jnp.where(group == place, take(block, index_down), down)
            row = (field * 4 + part) * ROWS
            to_upper[row : row + ROWS, :] = up
            to_lower[row : row + ROWS, :] = down


def copied(sources, targets, arrivals):
    return [
        pltpu.make_async_copy(source, target, arrivals.at[number])
        for number, (source, target) in enumerate(zip(sources, targets))
    ]


def pack_kernel(*refs):
    sources, (to_upper, to_lower, code_out), held, arrivals = refs[:5], refs[5:8], refs[8:13], refs[13]
    copies = copied(sources, held, arrivals)
    for number in (0, 4, 3, 1, 2):
        copies[number].start()
    copies[0].wait()

    def arrive(field):
        number = {10: 4, 9: 3, 0: 1, 3: 2}.get(field)
        if number is not None:
            copies[number].wait()

    pack_bricks(held[0], held[1:], to_upper, to_lower, code_out, arrive)


def remapper(code_ref, refs, lower, upper):
    lane = lane_of()
    code_of = code_ref[...]
    from_lower = code_of < BRICKS
    from_upper = code_of >= 2 * BRICKS
    index_own = (code_of % BRICKS) * BRICK + lane % BRICK

    def moved(field, tile):
        part, place = tile // 8, tile % 8
        index_in = place * BRICK + lane % BRICK
        row = (field * 4 + part) * ROWS
        own = take(field_block(refs, field, tile), index_own)
        low = take(lower[row : row + ROWS, :], index_in)
        high = take(upper[row : row + ROWS, :], index_in)
        return jnp.where(from_lower, low, jnp.where(from_upper, high, own))

    return moved


def tile_at(tile):
    half = tile % 2
    return tile // 2, slice(half * ROWS, (half + 1) * ROWS)


def remap_first_kernel(
    codes, velocity, history, pressure, void, lower, upper, press_out, void_out, to_upper, to_lower
):
    moved = remapper(codes, (velocity, history, pressure, void), lower, upper)
    for tile in range(32):
        layer, rows = tile_at(tile)
        press, void_new = moved(9, tile), moved(10, tile)
        press_out[layer, rows, :] = press
        void_out[layer, rows, :] = void_new
        for send, edge in ((to_lower, 0), (to_upper, EDGE - 1)):
            if layer == edge:
                for axis_no in range(3):
                    send[2 * HALO + axis_no, rows, :] = void_new * moved(axis_no, tile)
        if layer < HALO:
            to_lower[layer, rows, :] = void_new
            to_lower[HALO + layer, rows, :] = press
        if layer >= EDGE - HALO:
            to_upper[layer - EDGE + HALO, rows, :] = void_new
            to_upper[2 * HALO + layer - EDGE, rows, :] = press


def remap_rest_kernel(
    codes, velocity, history, pressure, void, lower, upper, flow_out, base_far, latest_far,
    base_out, latest_out, leaving,
):
    moved = remapper(codes, (velocity, history, pressure, void), lower, upper)
    copies = []
    for tile in range(32):
        layer, rows = tile_at(tile)
        for axis_no in range(3):
            flow, latest, older = [moved(axis_no + kind, tile) for kind in (0, 3, 6)]
            flow_out[axis_no, layer, rows, :] = flow
            latest_out[axis_no, layer, rows, :] = latest
            base_out[axis_no, layer, rows, :] = flow + TIME_STEP * (
                WEIGHT_OLDER * older - WEIGHT_LAST * latest
            )
        if tile % 8 == 7:
            part = pl.ds(tile // 8 * 4, 4)
            for source, target in ((base_out, base_far), (latest_out, latest_far)):
                copies.append(
                    pltpu.make_async_copy(source.at[:, part], target.at[:, part], leaving.at[len(copies)])
                )
                copies[-1].start()
    for copy in copies:
        copy.wait()


def pack_rows_kernel(flow, press, void, lower, upper, to_right, to_left):
    for send, rows, edge in ((to_right, slice(8, 16), EDGE - 1), (to_left, slice(0, 8), 0)):
        for number, own in ((0, void), (1, press)):
            start = number * WIDE * ROWS
            for layer in range(HALO):
                row = start + layer * ROWS
                send[row : row + ROWS, :] = lower[number * HALO + layer, rows, :]
                row = start + (HALO + EDGE + layer) * ROWS
                send[row : row + ROWS, :] = upper[number * HALO + layer, rows, :]
            for layer in range(EDGE):
                row = start + (HALO + layer) * ROWS
                send[row : row + ROWS, :] = own[layer, rows, :]
        for axis_no in range(3):
            row = 2 * WIDE * ROWS + axis_no * EDGE
            send[row : row + EDGE, :] = void[:, edge, :] * flow[axis_no, :, edge, :]


def split_two(value):
    high = value.astype(BF16)
    return high, (value - high.astype(F32)).astype(BF16)


NT = (((1,), (1,)), ((), ()))


def dispatch_kernel(records, owners, cells, out, shown, total):
    blocks = PARCELS // BLOCK
    owner_iota = lax.broadcasted_iota(jnp.int32, (OWNERS, BLOCK), 0).astype(F32).astype(BF16)
    before = (
        lax.broadcasted_iota(jnp.int32, (BLOCK, BLOCK), 0)
        < lax.broadcasted_iota(jnp.int32, (BLOCK, BLOCK), 1)
    ).astype(F32).astype(BF16)

    one, none = jnp.ones((2 * CAP, BLOCK), BF16), jnp.zeros((2 * CAP, BLOCK), BF16)

    def row_of(ref, block):
        return jnp.concatenate([ref[2 * block : 2 * block + 1, :], ref[2 * block + 1 : 2 * block + 2, :]], axis=1)

    for block in range(blocks):
        named = jnp.broadcast_to(row_of(owners, block).astype(F32), (OWNERS, BLOCK)).astype(BF16)
        shown[block * OWNERS : (block + 1) * OWNERS, :] = jnp.where(
            named == owner_iota, one[0:OWNERS, :], none[0:OWNERS, :]
        )
    earlier = lax.dot_general(
        shown[...], before, (((1,), (0,)), ((), ())), preferred_element_type=F32
    )
    base = jnp.zeros((OWNERS, 1), F32)
    row_iota = lax.broadcasted_iota(jnp.int32, (4, BLOCK), 0)
    key_iota = lax.broadcasted_iota(jnp.int32, (2 * CAP, BLOCK), 0).astype(F32).astype(BF16)
    for block in range(blocks):
        rows = slice(block * OWNERS, (block + 1) * OWNERS)
        hit = shown[rows, :].astype(F32)
        seen = earlier[block * OWNERS : (block + 1) * OWNERS, :]
        rank = jnp.sum(hit * (seen + base), axis=0, keepdims=True).astype(jnp.int32)
        base = base + seen[:, BLOCK - 1 : BLOCK] + hit[:, BLOCK - 1 : BLOCK]
        owner = row_of(owners, block)
        cell = row_of(cells, block)
        key = (owner // 32) * CAP + rank
        placed = jnp.where(
            jnp.broadcast_to(key.astype(F32), (2 * CAP, BLOCK)).astype(BF16) == key_iota, one, none
        )
        lanes = slice(block * BLOCK, (block + 1) * BLOCK)
        terms = jnp.zeros((4, BLOCK), F32)
        for size_class in range(4):
            state = records[4 * size_class : 4 * size_class + 4, lanes]
            coefficient = DRAG_SCALE * jnp.exp(state[3:4, :])
            terms = terms + coefficient * jnp.where(row_iota == 3, 1.0, state)
        depth, across, along = cell // 2048, (cell // LANES) % EDGE, cell % LANES
        major = (depth * 8 + across % 8).astype(F32)
        minor = ((across // 8) * LANES + along).astype(F32)
        blank2 = jnp.zeros((2, BLOCK), F32)
        blank4 = jnp.zeros((4, BLOCK), F32)
        coarse = terms.astype(BF16).astype(F32)
        values = jnp.concatenate(
            [coarse, major, minor, blank2, terms - coarse, blank4], axis=0
        ).astype(BF16)
        group = jnp.broadcast_to(owner % 32, (16, BLOCK)).astype(F32).astype(BF16)
        spread = jnp.concatenate(
            [jnp.where(group == jnp.asarray(number, BF16), values, jnp.zeros_like(values)) for number in range(32)],
            axis=0,
        )
        summed = lax.dot_general(spread, placed, NT, preferred_element_type=F32)
        if block == 0:
            total[...] = summed
        else:
            total[...] += summed
    for owner in range(OWNERS):
        row = (owner % 32) * 16
        lanes = slice((owner // 32) * CAP, (owner // 32 + 1) * CAP)
        out[owner, :, :] = total[row : row + 8, lanes] + total[row + 8 : row + 16, lanes]


def add_slots(arrived, sources, total, spread):
    iota_major = lax.broadcasted_iota(jnp.int32, (128, CAP), 0).astype(F32).astype(BF16)
    iota_minor = lax.broadcasted_iota(jnp.int32, (2 * LANES, CAP), 0).astype(F32).astype(BF16)
    zero = jnp.zeros((128, CAP), BF16)
    for start in sources:
        placed = []
        for place in range(STEP):
            slots = arrived[start + place, :, :]
            lanes = slice(place * CAP, (place + 1) * CAP)
            here = jnp.broadcast_to(slots[4:5, :], (128, CAP)).astype(BF16) == iota_major
            for channel in range(4):
                value = slots[channel : channel + 1, :]
                coarse = value.astype(BF16).astype(F32)
                for part, piece in ((0, coarse), (1, value - coarse)):
                    row = (channel * 2 + part) * 128
                    spread[row : row + 128, lanes] = jnp.where(
                        here, jnp.broadcast_to(piece, (128, CAP)).astype(BF16), zero
                    )
            minor = jnp.broadcast_to(slots[5:6, :], (2 * LANES, CAP)).astype(BF16)
            placed.append(jnp.where(minor == iota_minor, jnp.ones_like(minor), jnp.zeros_like(minor)))
        summed = lax.dot_general(
            spread[...], jnp.concatenate(placed, axis=1), NT, preferred_element_type=F32
        )
        if start == 0:
            total[...] = summed
        else:
            total[...] += summed


def deposit_kernel(arrived, out, total, spread):
    add_slots(arrived, range(0, OWNERS, STEP), total, spread)
    for channel in range(4):
        row = channel * 256
        for half in range(2):
            lanes = slice(half * LANES, (half + 1) * LANES)
            both = total[row : row + 128, lanes] + total[row + 128 : row + 256, lanes]
            out[channel, :, half * ROWS : (half + 1) * ROWS, :] = both.reshape(EDGE, ROWS, LANES)


def lane_up(value):
    lane = lax.broadcasted_iota(jnp.int32, value.shape, 1)
    return jnp.where(lane == LANES - 1, 0.0, pltpu.roll(value, LANES - 1, 1))


def lane_down(value):
    lane = lax.broadcasted_iota(jnp.int32, value.shape, 1)
    return jnp.where(lane == 0, 0.0, pltpu.roll(value, 1, 1))


def row_up(value, after):
    count = value.shape[0]
    row = lax.broadcasted_iota(jnp.int32, value.shape, 0)
    return jnp.where(row == count - 1, after, pltpu.roll(value, count - 1, 0))


def row_down(value, before):
    row = lax.broadcasted_iota(jnp.int32, value.shape, 0)
    return jnp.where(row == 0, before, pltpu.roll(value, 1, 0))


def has_neighbours():
    line = lax.axis_index("gx")
    return line > 0, line < lax.axis_size("gx") - 1


M_LOW = 2 * HALO
M_ROWS = 2 * WIDE * ROWS


def rate_kernel(
    flow, latest, base, void, lower, upper, left, right, deposit,
    history_out, trial_out, div_out, to_upper, to_lower, edge_out, scaled, rates, leaving,
):
    copies = [pltpu.make_async_copy(latest, history_out.at[1], leaving.at[0])]
    copies[0].start()
    def void_layer(layer):
        if layer < 0:
            return lower[HALO + layer, :, :]
        if layer >= EDGE:
            return upper[layer - EDGE, :, :]
        return void[layer, :, :]

    def moment_layer(axis_no, layer):
        if layer < 0:
            return lower[M_LOW + axis_no, :, :]
        if layer >= EDGE:
            return upper[M_LOW + axis_no, :, :]
        return void[layer, :, :] * flow[axis_no, layer, :, :]

    inside_left, inside_right = has_neighbours()
    for layer in range(EDGE):
        own = void[layer, :, :]
        row = (HALO + layer) * ROWS
        void_left = jnp.where(inside_left, left[row + ROWS - 1 : row + ROWS, :], 0.0)
        void_right = jnp.where(inside_right, right[row : row + 1, :], 0.0)
        near = (
            void_layer(layer + 1), void_layer(layer - 1),
            row_up(own, void_right), row_down(own, void_left),
            lane_up(own), lane_down(own),
        )
        around = near[0] + near[1] + near[2] + near[3] + near[4] + near[5]
        inverse = 1.0 / own
        drag = deposit[3, layer, :, :]
        slope = None
        for axis_no in range(3):
            mine = flow[axis_no, layer, :, :]
            moment = own * mine
            row = M_ROWS + axis_no * EDGE + layer
            summed = (
                moment_layer(axis_no, layer + 1) + moment_layer(axis_no, layer - 1)
                + row_up(moment, jnp.where(inside_right, right[row : row + 1, :], 0.0))
                + row_down(moment, jnp.where(inside_left, left[row : row + 1, :], 0.0))
                + lane_up(moment) + lane_down(moment)
            )
            rate = VISCOSITY * (summed - mine * around) + (
                deposit[axis_no, layer, :, :] - drag * mine
            ) * inverse
            rates[axis_no, layer, :, :] = rate
            trial = base[axis_no, layer, :, :] + (TIME_STEP * WEIGHT_NEW) * rate
            trial_out[axis_no, layer, :, :] = trial
            part = trial * (near[2 * axis_no] - near[2 * axis_no + 1])
            slope = part if axis_no == 0 else slope + part
            weighted = own * trial
            if axis_no == 0:
                scaled[layer, :, :] = weighted
            if axis_no == 1:
                slope = slope + row_up(weighted, 0.0) - row_down(weighted, 0.0)
                edge_out[0, layer : layer + 1, :] = weighted[0:1, :]
                edge_out[1, layer : layer + 1, :] = weighted[EDGE - 1 : EDGE, :]
            if axis_no == 2:
                slope = slope + lane_up(weighted) - lane_down(weighted)
        div_out[layer, :, :] = slope
        if layer % 4 == 3:
            part = pl.ds(layer - 3, 4)
            copies.append(
                pltpu.make_async_copy(
                    rates.at[:, part], history_out.at[0].at[:, part], leaving.at[len(copies)]
                )
            )
            copies[-1].start()
    for layer in range(EDGE):
        total = div_out[layer, :, :]
        if layer < EDGE - 1:
            total = total + scaled[layer + 1, :, :]
        if layer > 0:
            total = total - scaled[layer - 1, :, :]
        div_out[layer, :, :] = total
        if layer < REACH:
            to_lower[layer, :, :] = total
        if layer >= EDGE - REACH:
            to_upper[layer - EDGE + REACH, :, :] = total
    for send, layer, start in ((to_lower, 0, 0), (to_upper, EDGE - 1, EDGE - REACH)):
        send[REACH, :, :] = scaled[layer, :, :]
        for side in range(2):
            send[REACH + 1, side * 8 : side * 8 + REACH, :] = edge_out[side, start : start + REACH, :]
            send[REACH + 1, side * 8 + REACH : side * 8 + 8, :] = jnp.zeros((8 - REACH, LANES), F32)
    for copy in copies:
        copy.wait()


def pack_div_kernel(div, sent_lower, sent_upper, edge, lower, upper, wide_out, to_right, to_left):
    for layer in range(SPAN):
        if layer < REACH:
            value = lower[layer, :, :]
            if layer == REACH - 1:
                value = value + sent_lower[REACH, :, :]
        elif layer < REACH + EDGE:
            value = div[layer - REACH, :, :]
            if layer == REACH:
                value = value - lower[REACH, :, :]
            if layer == REACH + EDGE - 1:
                value = value + upper[REACH, :, :]
        else:
            value = upper[layer - REACH - EDGE, :, :]
            if layer == REACH + EDGE:
                value = value - sent_upper[REACH, :, :]
        wide_out[layer, :, :] = value
        row = layer * ROWS
        to_right[row : row + ROWS, :] = value[8:16, :]
        to_left[row : row + ROWS, :] = value[0:8, :]
    start = SPAN * ROWS
    for send, side in ((to_left, 0), (to_right, 1)):
        for layer in range(REACH):
            row = start + layer
            send[row : row + 1, :] = lower[REACH + 1, side * 8 + layer : side * 8 + layer + 1, :]
            row = start + REACH + EDGE + layer
            send[row : row + 1, :] = upper[REACH + 1, side * 8 + layer : side * 8 + layer + 1, :]
        for layer in range(EDGE):
            row = start + REACH + layer
            send[row : row + 1, :] = edge[side, layer : layer + 1, :]
        send[start + SPAN : start + 32, :] = jnp.zeros((32 - SPAN, LANES), F32)


def widen_kernel(press, void, lower, upper, left, right, void_wide, press_wide, factor):
    inside_left, inside_right = has_neighbours()
    for number, own, wide in ((0, void, void_wide), (1, press, press_wide)):
        for layer in range(WIDE):
            row = (number * WIDE + layer) * ROWS
            wide[layer, 0:8, :] = jnp.where(inside_left, left[row : row + ROWS, :], 0.0)
            wide[layer, 24:32, :] = jnp.where(inside_right, right[row : row + ROWS, :], 0.0)
            if layer < HALO:
                wide[layer, 8:24, :] = lower[number * HALO + layer, :, :]
            elif layer < HALO + EDGE:
                wide[layer, 8:24, :] = own[layer - HALO, :, :]
            else:
                wide[layer, 8:24, :] = upper[number * HALO + layer - HALO - EDGE, :, :]
    factor[0, :, :] = jnp.zeros((32, LANES), F32)
    factor[WIDE - 1, :, :] = jnp.zeros((32, LANES), F32)
    for layer in range(1, WIDE - 1):
        value = void_wide[layer, :, :]
        around = (
            void_wide[layer - 1, :, :] + void_wide[layer + 1, :, :]
            + row_up(value, 0.0) + row_down(value, 0.0) + lane_up(value) + lane_down(value)
        )
        outside = around <= 0.0
        factor[layer, :, :] = jnp.where(outside, 0.0, RELAXATION / jnp.where(outside, 1.0, around))


def relax_kernel(
    trial, void_wide, press_wide, factor, wide_div, sent_left, sent_right, left, right,
    velocity_out, pressure_out, press, known, first, second,
):
    inside_left, inside_right = has_neighbours()
    start = SPAN * ROWS
    for layer in range(SPAN):
        row = layer * ROWS
        edge = slice(start + layer, start + layer + 1)
        middle = wide_div[layer, :, :]
        west = left[row : row + ROWS, :]
        east = right[row : row + ROWS, :]
        block = jnp.concatenate([west, middle, east], axis=0)
        place = lax.broadcasted_iota(jnp.int32, (32, LANES), 0)
        block = block + jnp.where(place == 7, sent_left[edge, :], 0.0)
        block = block - jnp.where((place == 8) & inside_left, left[edge, :], 0.0)
        block = block + jnp.where((place == 23) & inside_right, right[edge, :], 0.0)
        block = block - jnp.where(place == 24, sent_right[edge, :], 0.0)
        known[layer + 1, :, :] = -2.0 * factor[layer + 1, :, :] * block
    for layer in range(WIDE):
        first[layer, :, :] = void_wide[layer, :, :] * press_wide[layer, :, :]
    for sweep in range(1, SWEEPS + 1):
        source, target = (first, second) if sweep % 2 == 1 else (second, first)
        before = press_wide if sweep == 1 else press
        for layer in range(sweep, WIDE - sweep):
            value = source[layer, :, :]
            around = (
                source[layer - 1, :, :] + source[layer + 1, :, :]
                + pltpu.roll(value, 31, 0) + pltpu.roll(value, 1, 0) + lane_up(value) + lane_down(value)
            )
            new = (
                (1.0 - RELAXATION) * before[layer, :, :] + known[layer, :, :]
                + factor[layer, :, :] * around
            )
            press[layer, :, :] = new
            if sweep < SWEEPS:
                target[layer, :, :] = void_wide[layer, :, :] * new
    half_step = 0.5 * TIME_STEP
    inner = slice(8, 24)
    for layer in range(HALO, HALO + EDGE):
        here = press[layer, :, :]
        void = void_wide[layer, :, :]
        centre = here[inner, :]
        pressure_out[layer - HALO, :, :] = centre

        def gradient(ahead, void_ahead, behind, void_behind):
            return void_ahead * (ahead - here) + void_behind * (here - behind)

        pieces = (
            gradient(press[layer + 1, :, :], void_wide[layer + 1, :, :], press[layer - 1, :, :], void_wide[layer - 1, :, :]),
            gradient(pltpu.roll(here, 31, 0), pltpu.roll(void, 31, 0), pltpu.roll(here, 1, 0), pltpu.roll(void, 1, 0)),
            gradient(lane_up(here), lane_up(void), lane_down(here), lane_down(void)),
        )
        for axis_no in range(3):
            velocity_out[axis_no, layer - HALO, :, :] = (
                trial[axis_no, layer - HALO, :, :] - half_step * pieces[axis_no][inner, :]
            )


def shifted(value, axis, steps):
    count = lax.axis_size(axis)
    return lax.ppermute(value, axis, [(source, (source + steps) % count) for source in range(count)])


def per_device(
    velocity, pressure, void_fraction, history, remap_list, parcel_records, parcel_owner, parcel_cells
):
    cells = pressure.shape
    codes = remap_list.transpose(1, 2, 0).reshape(-1, remap_list.shape[0])
    fields = (velocity, history, pressure, void_fraction)
    bricks = (FIELDS * 32, LANES)
    inputs = (codes,) + fields
    up, down, code_of = call(
        pack_kernel,
        [bricks, bricks, jax.ShapeDtypeStruct((ROWS, LANES), jnp.int32)],
        tuple(pltpu.with_memory_space_constraint(value, pltpu.HBM) for value in inputs),
        spaces={number: pltpu.HBM for number in range(len(inputs))},
        scratch=[(pltpu.SMEM if value is codes else pltpu.VMEM)(value.shape, value.dtype) for value in inputs]
        + [pltpu.SemaphoreType.DMA((len(inputs),))],
    )
    (outgoing,) = call(
        dispatch_kernel,
        [(OWNERS, 8, CAP)],
        (parcel_records, parcel_owner.reshape(32, 128), parcel_cells.reshape(32, 128)),
        scratch=(pltpu.VMEM((PARCELS // BLOCK * OWNERS, BLOCK), BF16), pltpu.VMEM((512, 2 * CAP), F32)),
    )
    brick_low = shifted(up, "gz", 1)
    brick_high = shifted(down, "gz", -1)
    arrived = lax.all_to_all(outgoing, "gz", split_axis=0, concat_axis=0, tiled=True)
    layers = (2 * HALO + 3, EDGE, LANES)
    remap_inputs = (code_of,) + fields + (brick_low, brick_high)
    press, void, up, down = call(remap_first_kernel, [cells, cells, layers, layers], remap_inputs)
    state_low = shifted(up, "gz", 1)
    state_high = shifted(down, "gz", -1)
    flow, base, latest = call(
        remap_rest_kernel,
        [(3,) + cells] * 3,
        remap_inputs,
        scratch=[pltpu.VMEM((3,) + cells, F32)] * 2 + [pltpu.SemaphoreType.DMA((8,))],
        far=(1, 2),
    )
    sums = (1024, 2 * LANES)
    spread = pltpu.VMEM((1024, STEP * CAP), BF16)
    rows = (2 * WIDE * ROWS + 3 * EDGE, LANES)
    right, left = call(
        pack_rows_kernel,
        [rows, rows],
        (flow, press, void, state_low, state_high),
    )
    (deposit,) = call(
        deposit_kernel, [(4,) + cells], (arrived,), scratch=(pltpu.VMEM(sums, F32), spread)
    )
    state_left = shifted(right, "gx", 1)
    state_right = shifted(left, "gx", -1)
    latest = pltpu.with_memory_space_constraint(latest, pltpu.HBM)
    new_history, trial, div, up, down, edge = call(
        rate_kernel,
        [(2, 3) + cells, (3,) + cells, cells, (REACH + 2,) + cells[1:], (REACH + 2,) + cells[1:], (2, EDGE, LANES)],
        (flow, latest, base, void, state_low, state_high, state_left, state_right, deposit),
        spaces={1: pltpu.HBM},
        scratch=(pltpu.VMEM(cells, F32), pltpu.VMEM((3,) + cells, F32), pltpu.SemaphoreType.DMA((5,))),
        far=(0,),
    )
    div_low = shifted(up, "gz", 1)
    div_high = shifted(down, "gz", -1)
    wide = (WIDE, 2 * EDGE, LANES)
    void_wide, press_wide, factor = call(
        widen_kernel, [wide, wide, wide], (press, void, state_low, state_high, state_left, state_right)
    )
    rows = (SPAN * ROWS + 32, LANES)
    wide_div, right, left = call(
        pack_div_kernel, [(SPAN, EDGE, LANES), rows, rows], (div, down, up, edge, div_low, div_high)
    )
    div_left = shifted(right, "gx", 1)
    div_right = shifted(left, "gx", -1)
    new_velocity, new_pressure = call(
        relax_kernel,
        [(3,) + cells, cells],
        (trial, void_wide, press_wide, factor, wide_div, left, right, div_left, div_right),
        scratch=[pltpu.VMEM(wide, F32) for _ in range(4)],
    )
    return new_velocity, new_pressure, new_history


def solution(mesh):
    return jax.shard_map(
        per_device,
        mesh=mesh,
        in_specs=(
            P(None, "gz", "gx", None),
            P("gz", "gx", None),
            P("gz", "gx", None),
            P(None, None, "gz", "gx", None),
            P(),
            P(None, ("gz", "gx")),
            P(("gz", "gx"), None),
            P(("gz", "gx")),
        ),
        out_specs=(P(None, "gz", "gx", None), P("gz", "gx", None), P(None, None, "gz", "gx", None)),
        check_vma=False,
    )
```

```python
import jax
import jax.numpy as jnp
from jax import lax
from jax.experimental import pallas as pl
from jax.experimental.pallas import tpu as pltpu
from jax.sharding import PartitionSpec as P

SWEEPS = 6
TIME_STEP = 0.25
VISCOSITY = 0.5
DRAG_SCALE = 0.5
RELAXATION = 0.8
WEIGHT_NEW = 23.0 / 12.0
WEIGHT_LAST = 16.0 / 12.0
WEIGHT_OLDER = 5.0 / 12.0

BRICK = 16
BRICKS = 8
EDGE = 16
LANES = 128
ROWS = 8
HALO = SWEEPS + 1
WIDE = HALO + EDGE + HALO
REACH = SWEEPS
SPAN = REACH + EDGE + REACH
FIELDS = 11
OWNERS = 64
CAP = 128
PARCELS = 4096
BLOCK = 256
STEP = 4
VMEM_LIMIT = 16 * 1024 * 1024

F32 = jnp.float32
BF16 = jnp.bfloat16


def call(kernel, outs, args, spaces=None, scratch=(), far=(), aliases=None):
    spaces = spaces or {}
    shapes = [out if isinstance(out, jax.ShapeDtypeStruct) else jax.ShapeDtypeStruct(out, F32) for out in outs]
    shapes = [
        pltpu.HBM(shape.shape, shape.dtype) if number in far else shape for number, shape in enumerate(shapes)
    ]
    return pl.pallas_call(
        kernel,
        out_shape=shapes,
        in_specs=[
            pl.BlockSpec(memory_space=spaces.get(number, pltpu.VMEM)) for number in range(len(args))
        ],
        out_specs=[
            pl.BlockSpec(memory_space=pltpu.HBM if number in far else pltpu.VMEM) for number in range(len(outs))
        ],
        input_output_aliases=aliases or {},
        scratch_shapes=list(scratch),
        compiler_params=pltpu.CompilerParams(vmem_limit_bytes=VMEM_LIMIT),
    )(*args)


def lane_of():
    return lax.broadcasted_iota(jnp.int32, (ROWS, LANES), 1)


def take(block, index):
    return jnp.take_along_axis(block, index, axis=1, mode="promise_in_bounds")


def field_block(refs, field, tile):
    velocity, history, pressure, void = refs
    layer, half = tile // 2, tile % 2
    rows = slice(half * ROWS, (half + 1) * ROWS)
    if field < 3:
        return velocity[field, layer, rows, :]
    if field < 9:
        return history[(field - 3) // 3, field % 3, layer, rows, :]
    return (pressure if field == 9 else void)[layer, rows, :]


def pack_bricks(codes, refs, to_upper, to_lower, code_out, arrive):
    cycle = lax.axis_index("gz")
    line = lax.axis_index("gx")
    size = lax.axis_size("gz")
    upper = lax.rem(cycle + 1, size)
    lower = lax.rem(cycle + size - 1, size)
    slot_up = jnp.int32(0)
    slot_down = jnp.int32(0)
    lane = lane_of()
    group = lane // BRICK
    code_of = jnp.zeros((ROWS, LANES), jnp.int32)
    for brick in range(BRICKS):
        code = codes[line * BRICKS + brick, upper]
        slot_up = slot_up + jnp.where(code < BRICKS, code, 0)
        code = codes[line * BRICKS + brick, lower]
        slot_down = slot_down + jnp.where(code >= 2 * BRICKS, code - 2 * BRICKS, 0)
        code_of = jnp.where(group == brick, codes[line * BRICKS + brick, cycle], code_of)
    code_out[...] = code_of
    index_up = slot_up * BRICK + lane % BRICK
    index_down = slot_down * BRICK + lane % BRICK
    for field in (10, 9, 0, 1, 2, 3, 4, 5, 6, 7, 8):
        arrive(field)
        for part in range(4):
            up = jnp.zeros((ROWS, LANES), F32)
            down = jnp.zeros((ROWS, LANES), F32)
            for place in range(8):
                block = field_block(refs, field, part * 8 + place)
                up = jnp.where(group == place, take(block, index_up), up)
                down = jnp.where(group == place, take(block, index_down), down)
            row = (field * 4 + part) * ROWS
            to_upper[row : row + ROWS, :] = up
            to_lower[row : row + ROWS, :] = down


def copied(sources, targets, arrivals):
    return [
        pltpu.make_async_copy(source, target, arrivals.at[number])
        for number, (source, target) in enumerate(zip(sources, targets))
    ]


def pack_kernel(*refs):
    sources, (to_upper, to_lower, code_out), held, arrivals = refs[:5], refs[5:8], refs[8:13], refs[13]
    copies = copied(sources, held, arrivals)
    for number in (0, 4, 3, 1, 2):
        copies[number].start()
    copies[0].wait()

    def arrive(field):
        number = {10: 4, 9: 3, 0: 1, 3: 2}.get(field)
        if number is not None:
            copies[number].wait()

    pack_bricks(held[0], held[1:], to_upper, to_lower, code_out, arrive)


def remapper(code_ref, refs, lower, upper):
    lane = lane_of()
    code_of = code_ref[...]
    from_lower = code_of < BRICKS
    from_upper = code_of >= 2 * BRICKS
    index_own = (code_of % BRICKS) * BRICK + lane % BRICK

    def moved(field, tile):
        part, place = tile // 8, tile % 8
        index_in = place * BRICK + lane % BRICK
        row = (field * 4 + part) * ROWS
        own = take(field_block(refs, field, tile), index_own)
        low = take(lower[row : row + ROWS, :], index_in)
        high = take(upper[row : row + ROWS, :], index_in)
        return jnp.where(from_lower, low, jnp.where(from_upper, high, own))

    return moved


def tile_at(tile):
    half = tile % 2
    return tile // 2, slice(half * ROWS, (half + 1) * ROWS)


def remap_first_kernel(
    codes, velocity, history, pressure, void, lower, upper, press_out, void_out, to_upper, to_lower
):
    moved = remapper(codes, (velocity, history, pressure, void), lower, upper)
    for tile in range(32):
        layer, rows = tile_at(tile)
        press, void_new = moved(9, tile), moved(10, tile)
        press_out[layer, rows, :] = press
        void_out[layer, rows, :] = void_new
        for send, edge in ((to_lower, 0), (to_upper, EDGE - 1)):
            if layer == edge:
                for axis_no in range(3):
                    send[2 * HALO + axis_no, rows, :] = void_new * moved(axis_no, tile)
        if layer < HALO:
            to_lower[layer, rows, :] = void_new
            to_lower[HALO + layer, rows, :] = press
        if layer >= EDGE - HALO:
            to_upper[layer - EDGE + HALO, rows, :] = void_new
            to_upper[2 * HALO + layer - EDGE, rows, :] = press


def remap_rest_kernel(
    codes, velocity, history, pressure, void, lower, upper, flow_out, base_far, latest_far,
    base_out, latest_out, leaving,
):
    moved = remapper(codes, (velocity, history, pressure, void), lower, upper)
    copies = []
    for tile in range(32):
        layer, rows = tile_at(tile)
        for axis_no in range(3):
            flow, latest, older = [moved(axis_no + kind, tile) for kind in (0, 3, 6)]
            flow_out[axis_no, layer, rows, :] = flow
            latest_out[axis_no, layer, rows, :] = latest
            base_out[axis_no, layer, rows, :] = flow + TIME_STEP * (
                WEIGHT_OLDER * older - WEIGHT_LAST * latest
            )
        if tile % 8 == 7:
            part = pl.ds(tile // 8 * 4, 4)
            for source, target in ((base_out, base_far), (latest_out, latest_far)):
                copies.append(
                    pltpu.make_async_copy(source.at[:, part], target.at[:, part], leaving.at[len(copies)])
                )
                copies[-1].start()
    for copy in copies:
        copy.wait()


def pack_rows_kernel(flow, press, void, lower, upper, to_right, to_left):
    for send, rows, edge in ((to_right, slice(8, 16), EDGE - 1), (to_left, slice(0, 8), 0)):
        for number, own in ((0, void), (1, press)):
            start = number * WIDE * ROWS
            for layer in range(HALO):
                row = start + layer * ROWS
                send[row : row + ROWS, :] = lower[number * HALO + layer, rows, :]
                row = start + (HALO + EDGE + layer) * ROWS
                send[row : row + ROWS, :] = upper[number * HALO + layer, rows, :]
            for layer in range(EDGE):
                row = start + (HALO + layer) * ROWS
                send[row : row + ROWS, :] = own[layer, rows, :]
        for axis_no in range(3):
            row = 2 * WIDE * ROWS + axis_no * EDGE
            send[row : row + EDGE, :] = void[:, edge, :] * flow[axis_no, :, edge, :]


def split_two(value):
    high = value.astype(BF16)
    return high, (value - high.astype(F32)).astype(BF16)


NT = (((1,), (1,)), ((), ()))


def dispatch_kernel(records, owners, cells, out, shown, total):
    blocks = PARCELS // BLOCK
    owner_iota = lax.broadcasted_iota(jnp.int32, (OWNERS, BLOCK), 0).astype(F32).astype(BF16)
    before = (
        lax.broadcasted_iota(jnp.int32, (BLOCK, BLOCK), 0)
        < lax.broadcasted_iota(jnp.int32, (BLOCK, BLOCK), 1)
    ).astype(F32).astype(BF16)

    one, none = jnp.ones((2 * CAP, BLOCK), BF16), jnp.zeros((2 * CAP, BLOCK), BF16)

    def row_of(ref, block):
        return jnp.concatenate([ref[2 * block : 2 * block + 1, :], ref[2 * block + 1 : 2 * block + 2, :]], axis=1)

    for block in range(blocks):
        named = jnp.broadcast_to(row_of(owners, block).astype(F32), (OWNERS, BLOCK)).astype(BF16)
        shown[block * OWNERS : (block + 1) * OWNERS, :] = jnp.where(
            named == owner_iota, one[0:OWNERS, :], none[0:OWNERS, :]
        )
    earlier = lax.dot_general(
        shown[...], before, (((1,), (0,)), ((), ())), preferred_element_type=F32
    )
    base = jnp.zeros((OWNERS, 1), F32)
    row_iota = lax.broadcasted_iota(jnp.int32, (4, BLOCK), 0)
    key_iota = lax.broadcasted_iota(jnp.int32, (2 * CAP, BLOCK), 0).astype(F32).astype(BF16)
    for block in range(blocks):
        rows = slice(block * OWNERS, (block + 1) * OWNERS)
        hit = shown[rows, :].astype(F32)
        seen = earlier[block * OWNERS : (block + 1) * OWNERS, :]
        rank = jnp.sum(hit * (seen + base), axis=0, keepdims=True).astype(jnp.int32)
        base = base + seen[:, BLOCK - 1 : BLOCK] + hit[:, BLOCK - 1 : BLOCK]
        owner = row_of(owners, block)
        cell = row_of(cells, block)
        key = (owner // 32) * CAP + rank
        placed = jnp.where(
            jnp.broadcast_to(key.astype(F32), (2 * CAP, BLOCK)).astype(BF16) == key_iota, one, none
        )
        lanes = slice(block * BLOCK, (block + 1) * BLOCK)
        terms = jnp.zeros((4, BLOCK), F32)
        for size_class in range(4):
            state = records[4 * size_class : 4 * size_class + 4, lanes]
            coefficient = DRAG_SCALE * jnp.exp(state[3:4, :])
            terms = terms + coefficient * jnp.where(row_iota == 3, 1.0, state)
        depth, across, along = cell // 2048, (cell // LANES) % EDGE, cell % LANES
        major = (depth * 8 + across % 8).astype(F32)
        minor = ((across // 8) * LANES + along).astype(F32)
        blank2 = jnp.zeros((2, BLOCK), F32)
        blank4 = jnp.zeros((4, BLOCK), F32)
        coarse = terms.astype(BF16).astype(F32)
        values = jnp.concatenate(
            [coarse, major, minor, blank2, terms - coarse, blank4], axis=0
        ).astype(BF16)
        group = jnp.broadcast_to(owner % 32, (16, BLOCK)).astype(F32).astype(BF16)
        spread = jnp.concatenate(
            [jnp.where(group == jnp.asarray(number, BF16), values, jnp.zeros_like(values)) for number in range(32)],
            axis=0,
        )
        summed = lax.dot_general(spread, placed, NT, preferred_element_type=F32)
        if block == 0:
            total[...] = summed
        else:
            total[...] += summed
    for owner in range(OWNERS):
        row = (owner % 32) * 16
        lanes = slice((owner // 32) * CAP, (owner // 32 + 1) * CAP)
        out[owner, :, :] = total[row : row + 8, lanes] + total[row + 8 : row + 16, lanes]


def add_slots(arrived, sources, total, spread):
    iota_major = lax.broadcasted_iota(jnp.int32, (128, CAP), 0).astype(F32).astype(BF16)
    iota_minor = lax.broadcasted_iota(jnp.int32, (2 * LANES, CAP), 0).astype(F32).astype(BF16)
    zero = jnp.zeros((128, CAP), BF16)
    for start in sources:
        placed = []
        for place in range(STEP):
            slots = arrived[start + place, :, :]
            lanes = slice(place * CAP, (place + 1) * CAP)
            here = jnp.broadcast_to(slots[4:5, :], (128, CAP)).astype(BF16) == iota_major
            for channel in range(4):
                value = slots[channel : channel + 1, :]
                coarse = value.astype(BF16).astype(F32)
                for part, piece in ((0, coarse), (1, value - coarse)):
                    row = (channel * 2 + part) * 128
                    spread[row : row + 128, lanes] = jnp.where(
                        here, jnp.broadcast_to(piece, (128, CAP)).astype(BF16), zero
                    )
            minor = jnp.broadcast_to(slots[5:6, :], (2 * LANES, CAP)).astype(BF16)
            placed.append(jnp.where(minor == iota_minor, jnp.ones_like(minor), jnp.zeros_like(minor)))
        summed = lax.dot_general(
            spread[...], jnp.concatenate(placed, axis=1), NT, preferred_element_type=F32
        )
        if start == 0:
            total[...] = summed
        else:
            total[...] += summed


def deposit_kernel(arrived, out, total, spread):
    add_slots(arrived, range(0, OWNERS, STEP), total, spread)
    for channel in range(4):
        row = channel * 256
        for half in range(2):
            lanes = slice(half * LANES, (half + 1) * LANES)
            both = total[row : row + 128, lanes] + total[row + 128 : row + 256, lanes]
            out[channel, :, half * ROWS : (half + 1) * ROWS, :] = both.reshape(EDGE, ROWS, LANES)


def lane_up(value):
    lane = lax.broadcasted_iota(jnp.int32, value.shape, 1)
    return jnp.where(lane == LANES - 1, 0.0, pltpu.roll(value, LANES - 1, 1))


def lane_down(value):
    lane = lax.broadcasted_iota(jnp.int32, value.shape, 1)
    return jnp.where(lane == 0, 0.0, pltpu.roll(value, 1, 1))


def row_up(value, after):
    count = value.shape[0]
    row = lax.broadcasted_iota(jnp.int32, value.shape, 0)
    return jnp.where(row == count - 1, after, pltpu.roll(value, count - 1, 0))


def row_down(value, before):
    row = lax.broadcasted_iota(jnp.int32, value.shape, 0)
    return jnp.where(row == 0, before, pltpu.roll(value, 1, 0))


def has_neighbours():
    line = lax.axis_index("gx")
    return line > 0, line < lax.axis_size("gx") - 1


M_LOW = 2 * HALO
M_ROWS = 2 * WIDE * ROWS


def rate_kernel(
    flow, latest, base, void, lower, upper, left, right, deposit,
    history_out, trial_out, div_out, to_upper, to_lower, edge_out, scaled, rates, held, leaving,
):
    arrival = pltpu.make_async_copy(latest, held, leaving.at[5])
    arrival.start()
    copies = [pltpu.make_async_copy(held, history_out.at[1], leaving.at[0])]
    def void_layer(layer):
        if layer < 0:
            return lower[HALO + layer, :, :]
        if layer >= EDGE:
            return upper[layer - EDGE, :, :]
        return void[layer, :, :]

    def moment_layer(axis_no, layer):
        if layer < 0:
            return lower[M_LOW + axis_no, :, :]
        if layer >= EDGE:
            return upper[M_LOW + axis_no, :, :]
        return void[layer, :, :] * flow[axis_no, layer, :, :]

    inside_left, inside_right = has_neighbours()
    for layer in range(EDGE):
        own = void[layer, :, :]
        row = (HALO + layer) * ROWS
        void_left = jnp.where(inside_left, left[row + ROWS - 1 : row + ROWS, :], 0.0)
        void_right = jnp.where(inside_right, right[row : row + 1, :], 0.0)
        near = (
            void_layer(layer + 1), void_layer(layer - 1),
            row_up(own, void_right), row_down(own, void_left),
            lane_up(own), lane_down(own),
        )
        around = near[0] + near[1] + near[2] + near[3] + near[4] + near[5]
        inverse = 1.0 / own
        drag = deposit[3, layer, :, :]
        slope = None
        for axis_no in range(3):
            mine = flow[axis_no, layer, :, :]
            moment = own * mine
            row = M_ROWS + axis_no * EDGE + layer
            summed = (
                moment_layer(axis_no, layer + 1) + moment_layer(axis_no, layer - 1)
                + row_up(moment, jnp.where(inside_right, right[row : row + 1, :], 0.0))
                + row_down(moment, jnp.where(inside_left, left[row : row + 1, :], 0.0))
                + lane_up(moment) + lane_down(moment)
            )
            rate = VISCOSITY * (summed - mine * around) + (
                deposit[axis_no, layer, :, :] - drag * mine
            ) * inverse
            rates[axis_no, layer, :, :] = rate
            trial = base[axis_no, layer, :, :] + (TIME_STEP * WEIGHT_NEW) * rate
            trial_out[axis_no, layer, :, :] = trial
            part = trial * (near[2 * axis_no] - near[2 * axis_no + 1])
            slope = part if axis_no == 0 else slope + part
            weighted = own * trial
            if axis_no == 0:
                scaled[layer, :, :] = weighted
            if axis_no == 1:
                slope = slope + row_up(weighted, 0.0) - row_down(weighted, 0.0)
                edge_out[0, layer : layer + 1, :] = weighted[0:1, :]
                edge_out[1, layer : layer + 1, :] = weighted[EDGE - 1 : EDGE, :]
            if axis_no == 2:
                slope = slope + lane_up(weighted) - lane_down(weighted)
        div_out[layer, :, :] = slope
        if layer % 4 == 3:
            part = pl.ds(layer - 3, 4)
            copies.append(
                pltpu.make_async_copy(
                    rates.at[:, part], history_out.at[0].at[:, part], leaving.at[len(copies)]
                )
            )
            copies[-1].start()
        if layer == 7:
            arrival.wait()
            copies[0].start()
    for layer in range(EDGE):
        total = div_out[layer, :, :]
        if layer < EDGE - 1:
            total = total + scaled[layer + 1, :, :]
        if layer > 0:
            total = total - scaled[layer - 1, :, :]
        div_out[layer, :, :] = total
        if layer < REACH:
            to_lower[layer, :, :] = total
        if layer >= EDGE - REACH:
            to_upper[layer - EDGE + REACH, :, :] = total
    for send, layer, start in ((to_lower, 0, 0), (to_upper, EDGE - 1, EDGE - REACH)):
        send[REACH, :, :] = scaled[layer, :, :]
        for side in range(2):
            send[REACH + 1, side * 8 : side * 8 + REACH, :] = edge_out[side, start : start + REACH, :]
            send[REACH + 1, side * 8 + REACH : side * 8 + 8, :] = jnp.zeros((8 - REACH, LANES), F32)
    for copy in copies:
        copy.wait()


def pack_div_kernel(div, sent_lower, sent_upper, edge, lower, upper, wide_out, to_right, to_left):
    for layer in range(SPAN):
        if layer < REACH:
            value = lower[layer, :, :]
            if layer == REACH - 1:
                value = value + sent_lower[REACH, :, :]
        elif layer < REACH + EDGE:
            value = div[layer - REACH, :, :]
            if layer == REACH:
                value = value - lower[REACH, :, :]
            if layer == REACH + EDGE - 1:
                value = value + upper[REACH, :, :]
        else:
            value = upper[layer - REACH - EDGE, :, :]
            if layer == REACH + EDGE:
                value = value - sent_upper[REACH, :, :]
        wide_out[layer, :, :] = value
        row = layer * ROWS
        to_right[row : row + ROWS, :] = value[8:16, :]
        to_left[row : row + ROWS, :] = value[0:8, :]
    start = SPAN * ROWS
    for send, side in ((to_left, 0), (to_right, 1)):
        for layer in range(REACH):
            row = start + layer
            send[row : row + 1, :] = lower[REACH + 1, side * 8 + layer : side * 8 + layer + 1, :]
            row = start + REACH + EDGE + layer
            send[row : row + 1, :] = upper[REACH + 1, side * 8 + layer : side * 8 + layer + 1, :]
        for layer in range(EDGE):
            row = start + REACH + layer
            send[row : row + 1, :] = edge[side, layer : layer + 1, :]
        send[start + SPAN : start + 32, :] = jnp.zeros((32 - SPAN, LANES), F32)


def widen_kernel(press, void, lower, upper, left, right, void_wide, press_wide, factor):
    inside_left, inside_right = has_neighbours()
    for number, own, wide in ((0, void, void_wide), (1, press, press_wide)):
        for layer in range(WIDE):
            row = (number * WIDE + layer) * ROWS
            wide[layer, 0:8, :] = jnp.where(inside_left, left[row : row + ROWS, :], 0.0)
            wide[layer, 24:32, :] = jnp.where(inside_right, right[row : row + ROWS, :], 0.0)
            if layer < HALO:
                wide[layer, 8:24, :] = lower[number * HALO + layer, :, :]
            elif layer < HALO + EDGE:
                wide[layer, 8:24, :] = own[layer - HALO, :, :]
            else:
                wide[layer, 8:24, :] = upper[number * HALO + layer - HALO - EDGE, :, :]
    factor[0, :, :] = jnp.zeros((32, LANES), F32)
    factor[WIDE - 1, :, :] = jnp.zeros((32, LANES), F32)
    for layer in range(1, WIDE - 1):
        value = void_wide[layer, :, :]
        around = (
            void_wide[layer - 1, :, :] + void_wide[layer + 1, :, :]
            + row_up(value, 0.0) + row_down(value, 0.0) + lane_up(value) + lane_down(value)
        )
        outside = around <= 0.0
        factor[layer, :, :] = jnp.where(outside, 0.0, RELAXATION / jnp.where(outside, 1.0, around))


def relax_kernel(
    trial, void_wide, press_wide, factor, wide_div, sent_left, sent_right, left, right,
    velocity_out, pressure_out, press, known, first, second,
):
    inside_left, inside_right = has_neighbours()
    start = SPAN * ROWS
    for layer in range(SPAN):
        row = layer * ROWS
        edge = slice(start + layer, start + layer + 1)
        middle = wide_div[layer, :, :]
        west = left[row : row + ROWS, :]
        east = right[row : row + ROWS, :]
        block = jnp.concatenate([west, middle, east], axis=0)
        place = lax.broadcasted_iota(jnp.int32, (32, LANES), 0)
        block = block + jnp.where(place == 7, sent_left[edge, :], 0.0)
        block = block - jnp.where((place == 8) & inside_left, left[edge, :], 0.0)
        block = block + jnp.where((place == 23) & inside_right, right[edge, :], 0.0)
        block = block - jnp.where(place == 24, sent_right[edge, :], 0.0)
        known[layer + 1, :, :] = -2.0 * factor[layer + 1, :, :] * block
    for layer in range(WIDE):
        first[layer, :, :] = void_wide[layer, :, :] * press_wide[layer, :, :]
    for sweep in range(1, SWEEPS + 1):
        source, target = (first, second) if sweep % 2 == 1 else (second, first)
        before = press_wide if sweep == 1 else press
        for layer in range(sweep, WIDE - sweep):
            value = source[layer, :, :]
            around = (
                source[layer - 1, :, :] + source[layer + 1, :, :]
                + pltpu.roll(value, 31, 0) + pltpu.roll(value, 1, 0) + lane_up(value) + lane_down(value)
            )
            new = (
                (1.0 - RELAXATION) * before[layer, :, :] + known[layer, :, :]
                + factor[layer, :, :] * around
            )
            press[layer, :, :] = new
            if sweep < SWEEPS:
                target[layer, :, :] = void_wide[layer, :, :] * new
    half_step = 0.5 * TIME_STEP
    inner = slice(8, 24)
    for layer in range(HALO, HALO + EDGE):
        here = press[layer, :, :]
        void = void_wide[layer, :, :]
        centre = here[inner, :]
        pressure_out[layer - HALO, :, :] = centre

        def gradient(ahead, void_ahead, behind, void_behind):
            return void_ahead * (ahead - here) + void_behind * (here - behind)

        pieces = (
            gradient(press[layer + 1, :, :], void_wide[layer + 1, :, :], press[layer - 1, :, :], void_wide[layer - 1, :, :]),
            gradient(pltpu.roll(here, 31, 0), pltpu.roll(void, 31, 0), pltpu.roll(here, 1, 0), pltpu.roll(void, 1, 0)),
            gradient(lane_up(here), lane_up(void), lane_down(here), lane_down(void)),
        )
        for axis_no in range(3):
            velocity_out[axis_no, layer - HALO, :, :] = (
                trial[axis_no, layer - HALO, :, :] - half_step * pieces[axis_no][inner, :]
            )


def shifted(value, axis, steps):
    count = lax.axis_size(axis)
    return lax.ppermute(value, axis, [(source, (source + steps) % count) for source in range(count)])


def per_device(
    velocity, pressure, void_fraction, history, remap_list, parcel_records, parcel_owner, parcel_cells
):
    cells = pressure.shape
    codes = remap_list.transpose(1, 2, 0).reshape(-1, remap_list.shape[0])
    fields = (velocity, history, pressure, void_fraction)
    bricks = (FIELDS * 32, LANES)
    inputs = (codes,) + fields
    up, down, code_of = call(
        pack_kernel,
        [bricks, bricks, jax.ShapeDtypeStruct((ROWS, LANES), jnp.int32)],
        tuple(pltpu.with_memory_space_constraint(value, pltpu.HBM) for value in inputs),
        spaces={number: pltpu.HBM for number in range(len(inputs))},
        scratch=[(pltpu.SMEM if value is codes else pltpu.VMEM)(value.shape, value.dtype) for value in inputs]
        + [pltpu.SemaphoreType.DMA((len(inputs),))],
    )
    (outgoing,) = call(
        dispatch_kernel,
        [(OWNERS, 8, CAP)],
        (parcel_records, parcel_owner.reshape(32, 128), parcel_cells.reshape(32, 128)),
        scratch=(pltpu.VMEM((PARCELS // BLOCK * OWNERS, BLOCK), BF16), pltpu.VMEM((512, 2 * CAP), F32)),
    )
    brick_low = shifted(up, "gz", 1)
    brick_high = shifted(down, "gz", -1)
    arrived = lax.all_to_all(outgoing, "gz", split_axis=0, concat_axis=0, tiled=True)
    layers = (2 * HALO + 3, EDGE, LANES)
    remap_inputs = (code_of,) + fields + (brick_low, brick_high)
    press, void, up, down = call(remap_first_kernel, [cells, cells, layers, layers], remap_inputs)
    state_low = shifted(up, "gz", 1)
    state_high = shifted(down, "gz", -1)
    flow, base, latest = call(
        remap_rest_kernel,
        [(3,) + cells] * 3,
        remap_inputs,
        scratch=[pltpu.VMEM((3,) + cells, F32)] * 2 + [pltpu.SemaphoreType.DMA((8,))],
        far=(1, 2),
    )
    sums = (1024, 2 * LANES)
    spread = pltpu.VMEM((1024, STEP * CAP), BF16)
    rows = (2 * WIDE * ROWS + 3 * EDGE, LANES)
    right, left = call(
        pack_rows_kernel,
        [rows, rows],
        (flow, press, void, state_low, state_high),
    )
    (deposit,) = call(
        deposit_kernel, [(4,) + cells], (arrived,), scratch=(pltpu.VMEM(sums, F32), spread)
    )
    state_left = shifted(right, "gx", 1)
    state_right = shifted(left, "gx", -1)
    latest = pltpu.with_memory_space_constraint(latest, pltpu.HBM)
    new_history, trial, div, up, down, edge = call(
        rate_kernel,
        [(2, 3) + cells, (3,) + cells, cells, (REACH + 2,) + cells[1:], (REACH + 2,) + cells[1:], (2, EDGE, LANES)],
        (flow, latest, base, void, state_low, state_high, state_left, state_right, deposit),
        spaces={1: pltpu.HBM},
        scratch=(pltpu.VMEM(cells, F32), pltpu.VMEM((3,) + cells, F32), pltpu.VMEM((3,) + cells, F32), pltpu.SemaphoreType.DMA((6,))),
        far=(0,),
    )
    div_low = shifted(up, "gz", 1)
    div_high = shifted(down, "gz", -1)
    wide = (WIDE, 2 * EDGE, LANES)
    void_wide, press_wide, factor = call(
        widen_kernel, [wide, wide, wide], (press, void, state_low, state_high, state_left, state_right)
    )
    rows = (SPAN * ROWS + 32, LANES)
    wide_div, right, left = call(
        pack_div_kernel, [(SPAN, EDGE, LANES), rows, rows], (div, down, up, edge, div_low, div_high)
    )
    div_left = shifted(right, "gx", 1)
    div_right = shifted(left, "gx", -1)
    new_velocity, new_pressure = call(
        relax_kernel,
        [(3,) + cells, cells],
        (trial, void_wide, press_wide, factor, wide_div, left, right, div_left, div_right),
        scratch=[pltpu.VMEM(wide, F32) for _ in range(4)],
    )
    return new_velocity, new_pressure, new_history


def solution(mesh):
    return jax.shard_map(
        per_device,
        mesh=mesh,
        in_specs=(
            P(None, "gz", "gx", None),
            P("gz", "gx", None),
            P("gz", "gx", None),
            P(None, None, "gz", "gx", None),
            P(),
            P(None, ("gz", "gx")),
            P(("gz", "gx"), None),
            P(("gz", "gx")),
        ),
        out_specs=(P(None, "gz", "gx", None), P("gz", "gx", None), P(None, None, "gz", "gx", None)),
        check_vma=False,
    )
```
